512 devices in a mesh: dp: 64 (over z_lo, y, core), mp: 8 (over z_hi, x).
Axes of the slice: x: 4, y: 8, z: 8 (z_hi: 2, z_lo: 4; z = z_hi * 4 + z_lo), core: 2. Of those that a mesh axis runs over, the one named last changes fastest.
Arguments:
- hidden_states: bfloat16 [32768, 2560], P('dp'), may hold values from -16 to 16
- head_weight: bfloat16 [2560, 1024], P(None, 'mp'), may hold values from -1 to 1
- agent_bias: float32 [8, 1024], P(None, 'mp'), may hold values from -6 to 6
- agent_ids: int32 [32768], P('dp'), may hold values from 0 to 7
- actions: int32 [32768], P('dp'), may hold values from 0 to 1023
- rewards: float32 [32768], P('dp'), may hold values from -18 to 18
- values: float32 [32768], P('dp'), may hold values from -6 to 6
- episode_start: int32 [32768], P('dp'), may hold values 0 or 1
- prior_ratio: float32 [32768], P('dp'), may hold values from 0.5 to 2
- sample_rows: int32 [131072], P('dp'), may hold values from 0 to 32767, as said below
Outputs:
- natural_step: float32 [2560, 1024], P(None, 'mp')
The draws below stay inside these ranges and needn't reach their ends.
Inputs may be any that keep to these rules, and one draw needn't show every extreme that they name: `sample_rows`: each aligned block of 2048 entries names rows of the matching block of 512 rows of hidden_states; a row may be named more than once.
All inputs are finite; a program needn't handle non-finite values. No bound on the sum of `episode_start` on one device may be relied on, other than what follows from the above.
Results may differ from the reference program's by a relative error of at most 0.003.
Values may be sent and summed in bfloat16 or wider, within the bound.
A program may use at most 64 MiB of HBM per device.

```python
import math
import jax
import jax.numpy as jnp
import numpy as np
from jax import lax

D = 2560
A = 1024
AGENTS = 8
SEQ_LEN = 64
ITERS = 2
TOK_DEV = 512
SAMP_DEV = 2048
TOKENS = 32768
SAMPLES = 131072


def shared_base(key):
    key_states, key_weights = jax.random.split(jax.random.fold_in(key, 11))
    states = jnp.clip(jax.random.normal(key_states, (TOKENS, D), jnp.float32), -6.0, 6.0)
    weights = jnp.clip(jax.random.normal(key_weights, (D, A), jnp.float32), -6.0, 6.0) / math.sqrt(D)
    return (states, weights)


def draw_hidden_states(key, part):
    states, weights = shared_base(key)
    return states.astype(jnp.bfloat16)


def draw_head_weight(key, part):
    states, weights = shared_base(key)
    return weights.astype(jnp.bfloat16)


def draw_rewards(key, part):
    positions = jnp.arange(TOKENS, dtype=jnp.int32)
    blocks = TOKENS // TOK_DEV
    scale = 1.0 + 2.0 * (positions // TOK_DEV).astype(jnp.float32) / max(blocks - 1, 1)
    reward_key = jax.random.fold_in(key, 23)
    base = jnp.clip(jax.random.normal(reward_key, (TOKENS,), jnp.float32), -6.0, 6.0)
    return base * scale


def draw_sample_rows(key, part):
    total = SAMP_DEV * (TOKENS // TOK_DEV)
    positions = jnp.arange(total, dtype=jnp.int32)
    owner = positions // SAMP_DEV
    offset = positions % SAMP_DEV
    within = jax.random.randint(jax.random.fold_in(key, 31), (total,), 0, TOK_DEV, dtype=jnp.int32)
    within = jnp.where(offset == 0, jnp.int32(0), within)
    within = jnp.where(offset == SAMP_DEV - 1, jnp.int32(TOK_DEV - 1), within)
    return owner * TOK_DEV + within


def plant(entries, rng, least, top_value):
    place = [jax.random.randint(jax.random.fold_in(rng, axis), (), 0, length) for axis, length in enumerate(entries.shape)]
    longest = entries.shape.index(max(entries.shape))
    beside = place[:longest] + [(place[longest] + 1) % entries.shape[longest]] + place[longest + 1:]
    return entries.at[tuple(place)].set(least).at[tuple(beside)].set(top_value)


def steps_of(key, shape, cuts, low, top_value):
    factor_of, own = 1.0, jax.random.fold_in(key, 6)
    for position, shards_of in cuts:
        heights = jnp.exp(jax.random.uniform(jax.random.fold_in(own, position), (shards_of,), jnp.float32, low / len(cuts), top_value / len(cuts)))
        factor_of = factor_of * jnp.repeat(heights, shape[position] // shards_of).reshape([-1 if axis == position else 1 for axis in range(len(shape))])
    return factor_of


def cumulative_ranks(count, slope):
    portions = [(1 << 20) // math.isqrt(rank ** slope) + 1 for rank in range(1, count + 1)]
    spread = 1 + sum(portions) // (1 << 30)
    return np.cumsum(np.array([max(1, weight // spread) for weight in portions]))


def ranked_ids(own_key, shape, number_of, slope):
    grid = cumulative_ranks(number_of, slope)
    ticket = jax.random.randint(jax.random.fold_in(own_key, 1), shape, 0, int(grid[number_of - 1]))
    rank = jnp.searchsorted(jnp.asarray(grid, jnp.int32), ticket, side="right")
    return jax.random.permutation(jax.random.fold_in(own_key, 2), number_of)[rank].astype(jnp.int32)


def gaussian(key, extent, deviation, bound, shards=(), kind=jnp.bfloat16):
    level = steps_of(key, extent, shards, -0.22, 0.18) if shards else 1.0
    values = jax.random.normal(key, extent, jnp.float32) * deviation * level
    return jnp.minimum(jnp.maximum(values, -bound), bound).astype(kind)


def setup_inputs(seed: int = 0) -> dict:
    key_list = jax.random.split(jax.random.key(seed), 11)
    hidden_states = draw_hidden_states(jax.random.fold_in(key_list[10], 71), 0)
    head_weight = draw_head_weight(jax.random.fold_in(key_list[10], 71), 0)
    agent_bias = gaussian(key_list[2], (AGENTS, A), 1.0, 6.0, ((1, 8),), jnp.float32)
    agent_ids = plant(jax.random.randint(key_list[3], (TOKENS,), 0, AGENTS), jax.random.fold_in(key_list[3], 1), 0, AGENTS - 1).astype(jnp.int32)
    actions = plant(ranked_ids(key_list[4], (TOKENS,), A, 2), jax.random.fold_in(key_list[4], 3), 0, A - 1).astype(jnp.int32)
    rewards = draw_rewards(jax.random.fold_in(key_list[10], 71), 0)
    values = gaussian(key_list[6], (TOKENS,), 1.0, 6.0, ((0, 64),), jnp.float32)
    episode_start = plant((jax.random.randint(key_list[7], (TOKENS,), 0, 16) < 1).astype(jnp.int32), jax.random.fold_in(key_list[7], 1), 0, 1)
    prior_ratio = jnp.clip(jnp.exp(math.log(2.0) - 1.3862944 * jax.random.uniform(key_list[8], (TOKENS,), jnp.float32) ** steps_of(key_list[8], (TOKENS,), ((0, 64),), -0.2, 0.2)), 0.5, 2.0)
    sample_rows = draw_sample_rows(jax.random.fold_in(key_list[10], 71), 0)
    return dict(hidden_states=hidden_states, head_weight=head_weight, agent_bias=agent_bias, agent_ids=agent_ids, actions=actions, rewards=rewards, values=values, episode_start=episode_start, prior_ratio=prior_ratio, sample_rows=sample_rows)


GAMMA = 0.99
TRACE_DECAY = 0.95
DAMPING = 0.001
RADIUS_SHARE = 0.001

def advantages(rewards, values, episode_start):
    reward_rows = rewards.reshape(-1, SEQ_LEN)
    value_rows = values.reshape(-1, SEQ_LEN)
    start_rows = episode_start.reshape(-1, SEQ_LEN)
    episode_end = jnp.concatenate([start_rows[:, 1:], jnp.ones_like(start_rows[:, :1])], axis=1)
    continues = (1 - episode_end).astype(jnp.float32)
    value_next = jnp.concatenate([value_rows[:, 1:], jnp.zeros_like(value_rows[:, :1])], axis=1)
    temporal = reward_rows + GAMMA * continues * value_next - value_rows

    def backward(running, inputs):
        error, keeps = inputs
        updated = error + GAMMA * TRACE_DECAY * keeps * running
        return (updated, updated)
    final_state, advantage = lax.scan(backward, jnp.zeros((reward_rows.shape[0],), jnp.float32), (temporal.T, continues.T), reverse=True)
    return advantage.T.reshape(-1)

def transpose_product(left, right):
    return lax.dot_general(left, right, (((0,), (0,)), ((), ())), preferred_element_type=jnp.float32)

def reference(hidden_states, head_weight, agent_bias, agent_ids, actions, rewards, values, episode_start, prior_ratio, sample_rows):
    advantage = advantages(rewards, values, episode_start)
    adv_mean = jnp.sum(advantage) / TOKENS
    weight = prior_ratio * (advantage - adv_mean) / TOKENS
    logits = jnp.dot(hidden_states, head_weight, preferred_element_type=jnp.float32) + agent_bias[agent_ids]
    row_peak = lax.optimization_barrier(jnp.max(logits, axis=1, keepdims=True))
    exponent = jnp.exp(logits - row_peak)
    probs = exponent / lax.optimization_barrier(jnp.sum(exponent, axis=1, keepdims=True))
    picked = (actions[:, None] == jnp.arange(A, dtype=jnp.int32)[None, :]).astype(jnp.float32)
    logit_grad = (weight[:, None] * (picked - probs)).astype(jnp.bfloat16)
    grad = transpose_product(hidden_states, logit_grad)
    sampled = hidden_states[sample_rows]
    sprobs = probs[sample_rows]

    def fisher_product(vector):
        lifted = jnp.dot(sampled, vector.astype(jnp.bfloat16), preferred_element_type=jnp.float32)
        centre = lax.optimization_barrier(jnp.sum(sprobs * lifted, axis=1, keepdims=True))
        weighted = (sprobs * (lifted - centre)).astype(jnp.bfloat16)
        return transpose_product(sampled, weighted) / SAMPLES + DAMPING * vector
    solution = jnp.zeros_like(grad)
    resid = grad
    direction = grad
    resid_sq = jnp.sum(resid * resid)
    quad = jnp.float32(0.0)
    for iteration in range(ITERS):
        fisher_image = fisher_product(direction)
        curvature = jnp.sum(direction * fisher_image)
        step_size = resid_sq / curvature
        solution = solution + step_size * direction
        resid = resid - step_size * fisher_image
        quad = quad + step_size * step_size * curvature
        resid_next = jnp.sum(resid * resid)
        direction = resid + resid_next / resid_sq * direction
        resid_sq = resid_next
    return solution * jnp.sqrt(D * A * RADIUS_SHARE / quad)
```

```python
import functools
import math

import jax
import jax.numpy as jnp
from jax import lax
from jax.experimental import pallas as pl
from jax.experimental.pallas import tpu as pltpu
from jax.sharding import PartitionSpec as P

D = 2560
A = 1024
AGENTS = 8
SEQ_LEN = 64
GAMMA = 0.99
TRACE_DECAY = 0.95
DAMPING = 0.001
RADIUS_SHARE = 0.001

MESH = pl.DeviceIdType.MESH
F32 = jnp.float32
BF16 = jnp.bfloat16
NY = 8
NZ = 4
NM = 8
ROWS = 512
SAMPLES = 2048
COLS = 128
QUARTER = D // NZ
FAR_FIRST = (4, 3, 5, 2, 6, 1, 7)
NEAR_FIRST = (1, 7, 2, 6, 3, 5, 4)


def kernel(
    hidden, head, bias, ids, actions, rewards, values, starts, ratio, samples,
    out,
    probs, logit_grad, part, grad, image,
    peak_box, centre_box, final_box, dots_m, dots_y, dots_q, adv_y, adv_q, curv_y, curv_q,
    core_box, sum_box, y_box, z_own, z_box,
    small_s, small_r, rs_core_s, rs_core_r, rs_y_s, rs_y_r, rs_z_s, rs_z_r,
    ag_z_s, ag_z_r, ag_y_s, ag_y_r, ag_c_s, ag_c_r,
):
    dp, me_m = lax.axis_index("dp"), lax.axis_index("mp")
    core = lax.rem(dp, 2)
    y = lax.rem(dp // 2, NY)
    z = dp // (2 * NY)
    q = z * 2 + core

    def at_y(k):
        return ((z * NY + k) * 2 + core, me_m)

    def at_q(k):
        return ((k // 2 * NY + y) * 2 + lax.rem(k, 2), me_m)

    def at_z(k):
        return ((k * NY + y) * 2 + core, me_m)

    def at_m(k):
        return (dp, k)

    other = (dp + 1 - 2 * core, me_m)

    barrier = pltpu.get_barrier_semaphore()
    for o in range(1, 8):
        for target in (
            at_y(lax.rem(y + o, NY)),
            at_q(lax.rem(q + o, 8)),
            at_m(lax.rem(me_m + o, NM)),
        ):
            pl.semaphore_signal(barrier, inc=1, device_id=target, device_id_type=MESH)
    pl.semaphore_wait(barrier, 21)

    def copy(src, dst, send, recv, target):
        return pltpu.make_async_remote_copy(
            src_ref=src, dst_ref=dst, send_sem=send, recv_sem=recv,
            device_id=target, device_id_type=MESH,
        )

    def swap_start(n, box, me, place):
        for o in range(1, 8):
            copy(
                box.at[me], box.at[me], small_s.at[n, o], small_r.at[n, me],
                place(lax.rem(me + o, 8)),
            ).start()

    def swap_wait(n, box, me, place):
        for o in range(1, 8):
            k = lax.rem(me + o, 8)
            c = copy(box.at[k], box.at[k], small_s.at[n, o], small_r.at[n, k], place(k))
            c.wait_send()
            c.wait_recv()

    def total(box):
        acc = box[0]
        for k in range(1, 8):
            acc = acc + box[k]
        return acc

    def lane_part(row):
        return row[:, 0:128] + row[:, 128:256] + row[:, 256:384] + row[:, 384:512]

    def ahead(x, s):
        return pltpu.roll(x, ROWS - s, 1)

    def wide(ref):
        return jnp.broadcast_to(ref[...].astype(F32), (8, ROWS))

    position = lax.broadcasted_iota(jnp.int32, (8, ROWS), 1)
    value = wide(values)
    ends = (lax.rem(position, SEQ_LEN) == SEQ_LEN - 1) | (ahead(wide(starts), 1) > 0.5)
    continues = jnp.where(ends, 0.0, 1.0)
    advantage = wide(rewards) + GAMMA * continues * ahead(value, 1) - value
    keeps = GAMMA * TRACE_DECAY * continues
    for s in (1, 2, 4, 8, 16, 32):
        advantage = advantage + keeps * ahead(advantage, s)
        keeps = keeps * ahead(keeps, s)
    advantage = advantage[0:1]
    adv_y[y] = lane_part(advantage)
    swap_start(0, adv_y, y, at_y)

    logits = jnp.dot(hidden[...], head[...], preferred_element_type=F32).T
    bias_t = bias[...].T
    agent = ids[...]
    for k in range(AGENTS):
        logits = logits + jnp.where(agent == k, bias_t[:, k : k + 1], 0.0)
    peak = jnp.max(logits, axis=0, keepdims=True)
    exponent = jnp.exp(logits - peak)
    peak_box[me_m, 0:1] = peak
    peak_box[me_m, 1:2] = jnp.sum(exponent, axis=0, keepdims=True)
    probs[...] = exponent
    swap_start(1, peak_box, me_m, at_m)

    swap_wait(0, adv_y, y, at_y)
    adv_q[q] = total(adv_y)
    swap_start(2, adv_q, q, at_q)

    local = samples[...] - dp * ROWS
    high = lax.shift_right_logical(local, 7)
    low = lax.bitwise_and(local, 127)
    high_hot = (lax.broadcasted_iota(jnp.int32, (8, SAMPLES), 0) == high).astype(F32).astype(BF16)
    low_hot = (lax.broadcasted_iota(jnp.int32, (128, SAMPLES), 0) == low).astype(F32).astype(BF16)
    tally = lax.dot_general(
        high_hot, low_hot, (((1,), (1,)), ((), ())), preferred_element_type=F32
    )
    count = jnp.concatenate([tally[0:1], tally[1:2], tally[2:3], tally[3:4]], axis=1)

    swap_wait(1, peak_box, me_m, at_m)
    row_peak = peak_box[0, 0:1]
    for k in range(1, NM):
        row_peak = jnp.maximum(row_peak, peak_box[k, 0:1])
    denominator = peak_box[0, 1:2] * jnp.exp(peak_box[0, 0:1] - row_peak)
    for k in range(1, NM):
        denominator = denominator + peak_box[k, 1:2] * jnp.exp(peak_box[k, 0:1] - row_peak)
    prob = probs[...] * (jnp.exp(peak - row_peak) / denominator)
    probs[...] = prob

    swap_wait(2, adv_q, q, at_q)
    tokens = ROWS * 64
    adv_mean = jnp.sum(total(adv_q), axis=1, keepdims=True) / tokens
    weight = ratio[...] * (advantage - adv_mean) / tokens
    picked = lax.broadcasted_iota(jnp.int32, (COLS, ROWS), 0) == actions[...] - me_m * COLS
    logit_grad[...] = (weight * (jnp.where(picked, 1.0, 0.0) - prob)).astype(BF16)

    def project():
        for j in range(5):
            cols = slice(512 * j, 512 * (j + 1))
            part[:, :, cols] = jnp.dot(
                logit_grad[...], hidden[:, cols], preferred_element_type=F32
            ).reshape(16, 8, 512)

    def scatter(n):
        sends = []
        for o in FAR_FIRST + (0,):
            c = copy(
                part.at[(1 - core) * 8 + lax.rem(y + o, NY)], core_box.at[n, o],
                rs_core_s.at[n, o], rs_core_r.at[n, o], other,
            )
            c.start()
            sends.append(c)
        for o in FAR_FIRST + (0,):
            k = lax.rem(y + o, NY)
            copy(
                part.at[core * 8 + k], core_box.at[n, o],
                rs_core_s.at[n, o], rs_core_r.at[n, o], other,
            ).wait_recv()
            sum_box[n, o] = part[core * 8 + k] + core_box[n, o]
            if o:
                c = copy(
                    sum_box.at[n, o], y_box.at[n, o], rs_y_s.at[n, o], rs_y_r.at[n, o], at_y(k)
                )
                c.start()
                sends.append(c)
        acc = sum_box[n, 0]
        for o in NEAR_FIRST:
            copy(
                sum_box.at[n, o], y_box.at[n, o], rs_y_s.at[n, o], rs_y_r.at[n, o],
                at_y(lax.rem(y + NY - o, NY)),
            ).wait_recv()
            acc = acc + y_box[n, o]
        for k in range(NZ):
            z_own[n, k] = acc[:, QUARTER * k : QUARTER * (k + 1)]
        for o in (3, 2, 1):
            k = lax.rem(z + o, NZ)
            c = copy(z_own.at[n, k], z_box.at[n, o], rs_z_s.at[n, o], rs_z_r.at[n, o], at_z(k))
            c.start()
            sends.append(c)
        shard = z_own[n, z]
        for o in (1, 2, 3):
            k = lax.rem(z + NZ - o, NZ)
            copy(
                z_own.at[n, k], z_box.at[n, o], rs_z_s.at[n, o], rs_z_r.at[n, o], at_z(k)
            ).wait_recv()
            shard = shard + z_box[n, o]
        for c in sends:
            c.wait_send()
        return shard

    columns = pl.ds(pl.multiple_of(z * QUARTER, 128), QUARTER)

    def gather_start(n, full):
        mine = core * 8 + y
        sends = []
        piece = full.at[mine, :, columns]
        for o in (3, 2, 1):
            c = copy(
                piece, piece, ag_z_s.at[n, o], ag_z_r.at[n, o], at_z(lax.rem(z + o, NZ))
            )
            c.start()
            sends.append(c)
        for o in (1, 2, 3):
            k = lax.rem(z + NZ - o, NZ)
            there = full.at[mine, :, pl.ds(pl.multiple_of(k * QUARTER, 128), QUARTER)]
            copy(there, there, ag_z_s.at[n, o], ag_z_r.at[n, o], at_z(k)).wait_recv()
        whole = full.at[mine]
        for o in FAR_FIRST:
            c = copy(
                whole, whole, ag_y_s.at[n, o], ag_y_r.at[n, o], at_y(lax.rem(y + o, NY))
            )
            c.start()
            sends.append(c)
        c = copy(whole, whole, ag_c_s.at[n, 0], ag_c_r.at[n, 0], other)
        c.start()
        sends.append(c)
        return sends

    def gather_wait(n, full, sends):
        for o in NEAR_FIRST:
            k = lax.rem(y + NY - o, NY)
            there = full.at[core * 8 + k]
            copy(there, there, ag_y_s.at[n, o], ag_y_r.at[n, o], at_y(k)).wait_recv()
            c = copy(there, there, ag_c_s.at[n, o], ag_c_r.at[n, o], other)
            c.start()
            sends.append(c)
        for o in (0,) + NEAR_FIRST:
            there = full.at[(1 - core) * 8 + lax.rem(y + NY - o, NY)]
            copy(there, there, ag_c_s.at[n, o], ag_c_r.at[n, o], other).wait_recv()
        for c in sends:
            c.wait_send()

    def lift(vector):
        return lax.dot_general(
            vector.reshape(COLS, D).astype(BF16), hidden[...], (((1,), (1,)), ((), ())),
            preferred_element_type=F32,
        )

    project()
    grad_piece = scatter(0)
    grad[core * 8 + y, :, columns] = grad_piece
    gather_wait(0, grad, gather_start(0, grad))

    lifted = lift(grad[...])
    prob = probs[...]
    centre_box[me_m] = jnp.sum(prob * lifted, axis=0, keepdims=True)
    swap_start(3, centre_box, me_m, at_m)
    swap_wait(3, centre_box, me_m, at_m)
    logit_grad[...] = (count * (prob * (lifted - total(centre_box)))).astype(BF16)
    project()
    image_piece = scatter(1) / (SAMPLES * 64) + DAMPING * grad_piece
    image[core * 8 + y, :, columns] = image_piece
    sends = gather_start(1, image)

    def folded(x):
        acc = x[:, 0:128]
        for k in range(1, 5):
            acc = acc + x[:, 128 * k : 128 * (k + 1)]
        return jnp.sum(acc, axis=0, keepdims=True)

    dots_m[me_m, 0:1] = folded(grad_piece * grad_piece)
    dots_m[me_m, 1:2] = folded(grad_piece * image_piece)
    dots_m[me_m, 2:3] = folded(image_piece * image_piece)
    dots_m[me_m, 3:8] = jnp.zeros((5, 128), F32)
    swap_start(4, dots_m, me_m, at_m)
    swap_wait(4, dots_m, me_m, at_m)
    dots_y[y] = total(dots_m)
    swap_start(5, dots_y, y, at_y)
    swap_wait(5, dots_y, y, at_y)
    dots_q[q] = total(dots_y)
    swap_start(6, dots_q, q, at_q)
    swap_wait(6, dots_q, q, at_q)
    dots = jnp.sum(total(dots_q), axis=1, keepdims=True)
    rr, curvature, image_sq = dots[0:1], dots[1:2], dots[2:3]
    step = rr / curvature
    rr_next = rr - 2.0 * step * curvature + step * step * image_sq
    beta = rr_next / rr
    quad = step * step * curvature
    gather_wait(1, image, sends)

    def direction():
        g = grad[...].reshape(COLS, D)
        return g, g - step * image[...].reshape(COLS, D) + beta * g

    lifted = lift(direction()[1])
    prob = probs[...]
    mass = jnp.sum(prob, axis=0, keepdims=True)
    moment = jnp.sum(prob * lifted, axis=0, keepdims=True)
    mean = jnp.where(mass > 0.0, moment / jnp.where(mass > 0.0, mass, 1.0), 0.0)
    spread = lifted - mean
    final_box[me_m, 0:1] = moment
    final_box[me_m, 1:2] = jnp.sum(prob * spread * spread, axis=0, keepdims=True)
    swap_start(7, final_box, me_m, at_m)
    swap_wait(7, final_box, me_m, at_m)
    sums = total(final_box)
    centre, variance = sums[0:1], sums[1:2]
    for k in range(NM):
        mass = peak_box[k, 1:2] * (jnp.exp(peak_box[k, 0:1] - row_peak) / denominator)
        mean = jnp.where(mass > 0.0, final_box[k, 0:1] / jnp.where(mass > 0.0, mass, 1.0), 0.0)
        variance = variance + mass * (mean - centre) * (mean - centre)
    curv_y[y] = lane_part(count * variance)
    swap_start(8, curv_y, y, at_y)
    swap_wait(8, curv_y, y, at_y)
    curv_q[q] = total(curv_y)
    swap_start(9, curv_q, q, at_q)
    swap_wait(9, curv_q, q, at_q)
    curvature = jnp.sum(total(curv_q), axis=1, keepdims=True) / (SAMPLES * 64)
    curvature = curvature + DAMPING * (rr_next + beta * beta * rr)
    last = rr_next / curvature
    quad = quad + last * last * curvature
    scale = jnp.sqrt(D * A * RADIUS_SHARE / quad)
    g, d = direction()
    out[...] = (step * g + last * d) * scale


def per_device(hidden, head, bias, ids, actions, rewards, values, starts, ratio, samples):
    dma = pltpu.SemaphoreType.DMA
    vmem = pltpu.VMEM

    def row(x):
        return x.reshape(1, -1)

    result = pl.pallas_call(
        kernel,
        out_shape=jax.ShapeDtypeStruct((COLS, D), F32),
        in_specs=[pl.BlockSpec(memory_space=pltpu.VMEM)] * 10,
        out_specs=pl.BlockSpec(memory_space=pltpu.VMEM),
        scratch_shapes=[
            vmem((COLS, ROWS), F32),
            vmem((COLS, ROWS), BF16),
            vmem((16, 8, D), F32),
            vmem((16, 8, D), F32),
            vmem((16, 8, D), F32),
            vmem((8, 2, ROWS), F32),
            vmem((8, 1, ROWS), F32),
            vmem((8, 2, ROWS), F32),
            vmem((8, 8, 128), F32),
            vmem((8, 8, 128), F32),
            vmem((8, 8, 128), F32),
            vmem((8, 1, 128), F32),
            vmem((8, 1, 128), F32),
            vmem((8, 1, 128), F32),
            vmem((8, 1, 128), F32),
            vmem((2, 8, 8, D), F32),
            vmem((2, 8, 8, D), F32),
            vmem((2, 8, 8, D), F32),
            vmem((2, NZ, 8, QUARTER), F32),
            vmem((2, NZ, 8, QUARTER), F32),
            dma((10, 8)),
            dma((10, 8)),
            dma((2, 8)),
            dma((2, 8)),
            dma((2, 8)),
            dma((2, 8)),
            dma((2, NZ)),
            dma((2, NZ)),
            dma((2, NZ)),
            dma((2, NZ)),
            dma((2, 8)),
            dma((2, 8)),
            dma((2, 8)),
            dma((2, 8)),
        ],
        compiler_params=pltpu.CompilerParams(
            collective_id=0, has_side_effects=True, vmem_limit_bytes=48 * 1024 * 1024
        ),
        name="step",
    )(
        hidden, head, bias, row(ids), row(actions), row(rewards), row(values), row(starts),
        row(ratio), row(samples),
    )
    return result.T


def solution(mesh):
    placed = (P("dp", None), P(None, "mp"), P(None, "mp")) + (P("dp"),) * 7
    return jax.shard_map(
        per_device, mesh=mesh, in_specs=placed, out_specs=P(None, "mp"), check_vma=False
    )
```

```python
import functools
import math

import jax
import jax.numpy as jnp
from jax import lax
from jax.experimental import pallas as pl
from jax.experimental.pallas import tpu as pltpu
from jax.sharding import PartitionSpec as P

D = 2560
A = 1024
AGENTS = 8
SEQ_LEN = 64
GAMMA = 0.99
TRACE_DECAY = 0.95
DAMPING = 0.001
RADIUS_SHARE = 0.001

MESH = pl.DeviceIdType.MESH
F32 = jnp.float32
BF16 = jnp.bfloat16
NY = 8
NZ = 4
NM = 8
ROWS = 512
SAMPLES = 2048
COLS = 128
LEFT = 1536
FAR_FIRST = (4, 3, 5, 2, 6, 1, 7)
NEAR_FIRST = (1, 7, 2, 6, 3, 5, 4)
CORE_ORDER = (
    ("a", 4), ("b", 3), ("a", 3), ("a", 5), ("b", 1), ("a", 2), ("a", 6), ("b", 2),
    ("a", 1), ("a", 7), ("a", 0), ("b", 0),
)


def kernel(
    hidden_in, head_in, bias_in, ids_in, actions_in, rewards_in, values_in, starts_in, ratio_in, samples_in,
    out,
    hidden, head, bias, ids, actions, rewards, values, starts, ratio, samples, loads,
    probs, logit_grad, part, grad_hi, grad_lo, image_hi,
    peak_box, centre_box, final_box, dots_m, dots_y, dots_q, adv_y, adv_q, curv_y, curv_q,
    core_a, core_b, send_a32, send_b32, y_a32, z_b32, send_a16, send_b16, y_a16, z_b16,
    own_a, own_b, z_a, y_b,
    small_s, small_r, rs_s, rs_r, ag_s, ag_r,
):
    fetches = [
        pltpu.make_async_copy(src, dst, loads.at[k])
        for k, (src, dst) in enumerate(
            (
                (rewards_in, rewards), (values_in, values), (starts_in, starts),
                (hidden_in, hidden), (head_in, head), (bias_in, bias), (ids_in, ids),
                (actions_in, actions), (ratio_in, ratio), (samples_in, samples),
            )
        )
    ]
    for fetch in fetches:
        fetch.start()

    dp, me_m = lax.axis_index("dp"), lax.axis_index("mp")
    core = lax.rem(dp, 2)
    y = lax.rem(dp // 2, NY)
    z = dp // (2 * NY)
    q = z * 2 + core

    def at_y(k):
        return ((z * NY + k) * 2 + core, me_m)

    def at_q(k):
        return ((k // 2 * NY + y) * 2 + lax.rem(k, 2), me_m)

    def at_z(k):
        return ((k * NY + y) * 2 + core, me_m)

    def at_m(k):
        return (dp, k)

    other = (dp + 1 - 2 * core, me_m)

    barrier = pltpu.get_barrier_semaphore()
    for o in range(1, 8):
        for target in (
            at_y(lax.rem(y + o, NY)),
            at_q(lax.rem(q + o, 8)),
            at_m(lax.rem(me_m + o, NM)),
        ):
            pl.semaphore_signal(barrier, inc=1, device_id=target, device_id_type=MESH)
    pl.semaphore_wait(barrier, 21)

    def copy(src, dst, send, recv, target):
        return pltpu.make_async_remote_copy(
            src_ref=src, dst_ref=dst, send_sem=send, recv_sem=recv,
            device_id=target, device_id_type=MESH,
        )

    def swap_start(n, box, me, place):
        for o in range(1, 8):
            copy(
                box.at[me], box.at[me], small_s.at[n, o], small_r.at[n, me],
                place(lax.rem(me + o, 8)),
            ).start()

    def swap_wait(n, box, me, place):
        for o in range(1, 8):
            k = lax.rem(me + o, 8)
            c = copy(box.at[k], box.at[k], small_s.at[n, o], small_r.at[n, k], place(k))
            c.wait_send()
            c.wait_recv()

    def total(box):
        acc = box[0]
        for k in range(1, 8):
            acc = acc + box[k]
        return acc

    def lane_part(row):
        return row[:, 0:128] + row[:, 128:256] + row[:, 256:384] + row[:, 384:512]

    for fetch in fetches[:3]:
        fetch.wait()

    def ahead(x, s):
        return pltpu.roll(x, ROWS - s, 1)

    def wide(ref):
        return jnp.broadcast_to(ref[...].astype(F32), (8, ROWS))

    position = lax.broadcasted_iota(jnp.int32, (8, ROWS), 1)
    value = wide(values)
    ends = (lax.rem(position, SEQ_LEN) == SEQ_LEN - 1) | (ahead(wide(starts), 1) > 0.5)
    continues = jnp.where(ends, 0.0, 1.0)
    advantage = wide(rewards) + GAMMA * continues * ahead(value, 1) - value
    keeps = GAMMA * TRACE_DECAY * continues
    for s in (1, 2, 4, 8, 16, 32):
        advantage = advantage + keeps * ahead(advantage, s)
        keeps = keeps * ahead(keeps, s)
    advantage = advantage[0:1]
    adv_y[y] = lane_part(advantage)
    swap_start(0, adv_y, y, at_y)

    for fetch in fetches[3:]:
        fetch.wait()

    logits = jnp.dot(hidden[...], head[...], preferred_element_type=F32).T
    bias_t = bias[...].T
    agent = ids[...]
    for k in range(AGENTS):
        logits = logits + jnp.where(agent == k, bias_t[:, k : k + 1], 0.0)
    peak = jnp.max(logits, axis=0, keepdims=True)
    exponent = jnp.exp(logits - peak)
    peak_box[me_m, 0:1] = peak
    peak_box[me_m, 1:2] = jnp.sum(exponent, axis=0, keepdims=True)
    probs[...] = exponent
    swap_start(1, peak_box, me_m, at_m)

    swap_wait(0, adv_y, y, at_y)
    adv_q[q] = total(adv_y)
    swap_start(2, adv_q, q, at_q)

    local = samples[...] - dp * ROWS
    high = lax.shift_right_logical(local, 7)
    low = lax.bitwise_and(local, 127)
    high_hot = (lax.broadcasted_iota(jnp.int32, (8, SAMPLES), 0) == high).astype(F32).astype(BF16)
    low_hot = (lax.broadcasted_iota(jnp.int32, (128, SAMPLES), 0) == low).astype(F32).astype(BF16)
    tally = lax.dot_general(
        high_hot, low_hot, (((1,), (1,)), ((), ())), preferred_element_type=F32
    )
    count = jnp.concatenate([tally[0:1], tally[1:2], tally[2:3], tally[3:4]], axis=1)

    swap_wait(1, peak_box, me_m, at_m)
    row_peak = peak_box[0, 0:1]
    for k in range(1, NM):
        row_peak = jnp.maximum(row_peak, peak_box[k, 0:1])
    denominator = peak_box[0, 1:2] * jnp.exp(peak_box[0, 0:1] - row_peak)
    for k in range(1, NM):
        denominator = denominator + peak_box[k, 1:2] * jnp.exp(peak_box[k, 0:1] - row_peak)
    prob = probs[...] * (jnp.exp(peak - row_peak) / denominator)
    probs[...] = prob

    swap_wait(2, adv_q, q, at_q)
    tokens = ROWS * 64
    adv_mean = jnp.sum(total(adv_q), axis=1, keepdims=True) / tokens
    weight = ratio[...] * (advantage - adv_mean) / tokens
    picked = lax.broadcasted_iota(jnp.int32, (COLS, ROWS), 0) == actions[...] - me_m * COLS
    logit_grad[...] = (weight * (jnp.where(picked, 1.0, 0.0) - prob)).astype(BF16)

    def project():
        for j in range(5):
            cols = slice(512 * j, 512 * (j + 1))
            part[:, :, cols] = jnp.dot(
                logit_grad[...], hidden[:, cols], preferred_element_type=F32
            ).reshape(16, 8, 512)

    def scatter(n, send_a, send_b, y_a, z_b):
        def core_copy(kind, o):
            if kind == "a":
                k = (1 - core) * 8 + lax.rem(y + o, NY)
                return copy(
                    part.at[k, :, 0:LEFT], core_a.at[n, o], rs_s.at[n, 0, o], rs_r.at[n, 0, o], other
                )
            k = (1 - core) * 8 + lax.rem(z + o, NZ) * 2
            return copy(
                part.at[pl.ds(k, 2), :, LEFT:D], core_b.at[n, o],
                rs_s.at[n, 1, o], rs_r.at[n, 1, o], other,
            )

        def leg_a(o, k):
            return copy(send_a.at[o], y_a.at[o], rs_s.at[n, 2, o], rs_r.at[n, 2, o], at_y(k))

        def leg_b(o, k):
            return copy(send_b.at[o], z_b.at[o], rs_s.at[n, 3, o], rs_r.at[n, 3, o], at_z(k))

        sends = []
        for kind, o in CORE_ORDER:
            c = core_copy(kind, o)
            c.start()
            sends.append(c)
        for kind, o in CORE_ORDER:
            core_copy(kind, o).wait_recv()
            if kind == "a":
                k = lax.rem(y + o, NY)
                term = part[core * 8 + k, :, 0:LEFT] + core_a[n, o]
                if o == 0:
                    acc_a = term
                    continue
                send_a[o] = term.astype(send_a.dtype)
                c = leg_a(o, k)
            else:
                k = lax.rem(z + o, NZ)
                term = part[pl.ds(core * 8 + 2 * k, 2), :, LEFT:D] + core_b[n, o]
                if o == 0:
                    acc_b = term
                    continue
                send_b[o] = term.astype(send_b.dtype)
                c = leg_b(o, k)
            c.start()
            sends.append(c)
        for o in (1, 2, 3):
            leg_b(o, lax.rem(z + NZ - o, NZ)).wait_recv()
            acc_b = acc_b + z_b[o].astype(F32)
        for k in range(NY):
            own_b[n, k] = acc_b[k // 4, :, 256 * (k % 4) : 256 * (k % 4 + 1)]
        for o in FAR_FIRST:
            k = lax.rem(y + o, NY)
            c = copy(own_b.at[n, k], y_b.at[n, o], rs_s.at[n, 4, o], rs_r.at[n, 4, o], at_y(k))
            c.start()
            sends.append(c)
        for o in NEAR_FIRST:
            leg_a(o, lax.rem(y + NY - o, NY)).wait_recv()
            acc_a = acc_a + y_a[o].astype(F32)
        for k in range(NZ):
            own_a[n, k] = acc_a[:, 384 * k : 384 * (k + 1)]
        for o in (3, 2, 1):
            k = lax.rem(z + o, NZ)
            c = copy(own_a.at[n, k], z_a.at[n, o], rs_s.at[n, 5, o], rs_r.at[n, 5, o], at_z(k))
            c.start()
            sends.append(c)
        shard_b = own_b[n, y]
        for o in NEAR_FIRST:
            k = lax.rem(y + NY - o, NY)
            copy(
                own_b.at[n, k], y_b.at[n, o], rs_s.at[n, 4, o], rs_r.at[n, 4, o], at_y(k)
            ).wait_recv()
            shard_b = shard_b + y_b[n, o]
        shard_a = own_a[n, z]
        for o in (1, 2, 3):
            k = lax.rem(z + NZ - o, NZ)
            copy(
                own_a.at[n, k], z_a.at[n, o], rs_s.at[n, 5, o], rs_r.at[n, 5, o], at_z(k)
            ).wait_recv()
            shard_a = shard_a + z_a[n, o]
        for c in sends:
            c.wait_send()
        return shard_a, shard_b

    def spot_a(full, ky, kz):
        return full.at[core * 8 + ky, :, pl.ds(pl.multiple_of(kz * 384, 128), 384)]

    def spot_b(full, ky, kz):
        columns = pl.ds(pl.multiple_of(LEFT + lax.rem(ky, 4) * 256, 128), 256)
        return full.at[core * 8 + 2 * kz + ky // 4, :, columns]

    def line_a(full, kc, ky):
        return full.at[kc * 8 + ky, :, 0:LEFT]

    def line_b(full, kc, kz):
        return full.at[pl.ds(kc * 8 + 2 * kz, 2), :, LEFT:D]

    def gather_start(n, full):
        sends = []

        def begin(ref, kind, o, target):
            c = copy(ref, ref, ag_s.at[n, kind, o], ag_r.at[n, kind, o], target)
            c.start()
            sends.append(c)

        for o in (3, 2, 1):
            begin(spot_a(full, y, z), 0, o, at_z(lax.rem(z + o, NZ)))
        for o in FAR_FIRST:
            begin(spot_b(full, y, z), 1, o, at_y(lax.rem(y + o, NY)))
        for o in (1, 2, 3):
            k = lax.rem(z + NZ - o, NZ)
            there = spot_a(full, y, k)
            copy(there, there, ag_s.at[n, 0, o], ag_r.at[n, 0, o], at_z(k)).wait_recv()
        for o in FAR_FIRST:
            begin(line_a(full, core, y), 2, o, at_y(lax.rem(y + o, NY)))
        begin(line_a(full, core, y), 4, 0, other)
        for o in NEAR_FIRST:
            k = lax.rem(y + NY - o, NY)
            there = spot_b(full, k, z)
            copy(there, there, ag_s.at[n, 1, o], ag_r.at[n, 1, o], at_y(k)).wait_recv()
        for o in (3, 2, 1):
            begin(line_b(full, core, z), 3, o, at_z(lax.rem(z + o, NZ)))
        begin(line_b(full, core, z), 5, 0, other)
        return sends

    def gather_wait(n, full, sends):
        def arrive(ref, kind, o, source, onward):
            copy(ref, ref, ag_s.at[n, kind, o], ag_r.at[n, kind, o], source).wait_recv()
            if onward:
                c = copy(ref, ref, ag_s.at[n, onward, o], ag_r.at[n, onward, o], other)
                c.start()
                sends.append(c)

        for kind, o in (("a", 1), ("a", 7), ("b", 1), ("a", 2), ("a", 6), ("b", 2), ("b", 3), ("a", 3), ("a", 5), ("a", 4)):
            if kind == "a":
                k = lax.rem(y + NY - o, NY)
                arrive(line_a(full, core, k), 2, o, at_y(k), 4)
            else:
                k = lax.rem(z + NZ - o, NZ)
                arrive(line_b(full, core, k), 3, o, at_z(k), 5)
        for o in range(NY):
            arrive(line_a(full, 1 - core, lax.rem(y + NY - o, NY)), 4, o, other, 0)
        for o in range(NZ):
            arrive(line_b(full, 1 - core, lax.rem(z + NZ - o, NZ)), 5, o, other, 0)
        for c in sends:
            c.wait_send()

    def keep(full, shards):
        shard_a, shard_b = shards
        full[core * 8 + y, :, pl.ds(pl.multiple_of(z * 384, 128), 384)] = shard_a.astype(BF16)
        columns = pl.ds(pl.multiple_of(LEFT + lax.rem(y, 4) * 256, 128), 256)
        full[core * 8 + 2 * z + y // 4, :, columns] = shard_b.astype(BF16)

    def lift(vector):
        return lax.dot_general(
            vector.reshape(COLS, D).astype(BF16), hidden[...], (((1,), (1,)), ((), ())),
            preferred_element_type=F32,
        )

    project()
    grad_piece = scatter(0, send_a32, send_b32, y_a32, z_b32)
    keep(grad_hi, grad_piece)
    keep(grad_lo, [x - x.astype(BF16).astype(F32) for x in grad_piece])
    gather_wait(0, grad_hi, gather_start(0, grad_hi))

    lifted = lift(grad_hi[...].astype(F32))
    prob = probs[...]
    centre_box[me_m] = jnp.sum(prob * lifted, axis=0, keepdims=True)
    swap_start(3, centre_box, me_m, at_m)
    swap_wait(3, centre_box, me_m, at_m)
    logit_grad[...] = (count * (prob * (lifted - total(centre_box)))).astype(BF16)
    project()
    fisher = [x / (SAMPLES * 64) for x in scatter(1, send_a16, send_b16, y_a16, z_b16)]
    keep(image_hi, fisher)
    image_piece = [f + DAMPING * g for f, g in zip(fisher, grad_piece)]
    sends = gather_start(1, image_hi)

    def folded(left, right):
        terms = [
            l[:, k : k + 128] * r[:, k : k + 128]
            for l, r in zip(left, right)
            for k in range(0, l.shape[1], 128)
        ]
        return jnp.sum(sum(terms[1:], terms[0]), axis=0, keepdims=True)

    dots_m[me_m, 0:1] = folded(grad_piece, grad_piece)
    dots_m[me_m, 1:2] = folded(grad_piece, image_piece)
    dots_m[me_m, 2:3] = folded(image_piece, image_piece)
    dots_m[me_m, 3:8] = jnp.zeros((5, 128), F32)
    swap_start(4, dots_m, me_m, at_m)
    swap_wait(4, dots_m, me_m, at_m)
    dots_y[y] = total(dots_m)
    swap_start(5, dots_y, y, at_y)
    swap_wait(5, dots_y, y, at_y)
    dots_q[q] = total(dots_y)
    swap_start(6, dots_q, q, at_q)
    swap_wait(6, dots_q, q, at_q)
    dots = jnp.sum(total(dots_q), axis=1, keepdims=True)
    rr, curvature, image_sq = dots[0:1], dots[1:2], dots[2:3]
    step = rr / curvature
    rr_next = rr - 2.0 * step * curvature + step * step * image_sq
    beta = rr_next / rr
    quad = step * step * curvature
    gather_wait(1, image_hi, sends)

    def direction(g):
        return g - step * (image_hi[...].astype(F32) + DAMPING * g) + beta * g

    lifted = lift(direction(grad_hi[...].astype(F32)))
    prob = probs[...]
    mass = jnp.sum(prob, axis=0, keepdims=True)
    moment = jnp.sum(prob * lifted, axis=0, keepdims=True)
    mean = jnp.where(mass > 0.0, moment / jnp.where(mass > 0.0, mass, 1.0), 0.0)
    spread = lifted - mean
    final_box[me_m, 0:1] = moment
    final_box[me_m, 1:2] = jnp.sum(prob * spread * spread, axis=0, keepdims=True)
    swap_start(7, final_box, me_m, at_m)
    sends = gather_start(2, grad_lo)
    swap_wait(7, final_box, me_m, at_m)
    sums = total(final_box)
    centre, variance = sums[0:1], sums[1:2]
    for k in range(NM):
        mass = peak_box[k, 1:2] * (jnp.exp(peak_box[k, 0:1] - row_peak) / denominator)
        mean = jnp.where(mass > 0.0, final_box[k, 0:1] / jnp.where(mass > 0.0, mass, 1.0), 0.0)
        variance = variance + mass * (mean - centre) * (mean - centre)
    curv_y[y] = lane_part(count * variance)
    swap_start(8, curv_y, y, at_y)
    swap_wait(8, curv_y, y, at_y)
    curv_q[q] = total(curv_y)
    swap_start(9, curv_q, q, at_q)
    gather_wait(2, grad_lo, sends)
    swap_wait(9, curv_q, q, at_q)
    curvature = jnp.sum(total(curv_q), axis=1, keepdims=True) / (SAMPLES * 64)
    curvature = curvature + DAMPING * (rr_next + beta * beta * rr)
    last = rr_next / curvature
    quad = quad + last * last * curvature
    scale = jnp.sqrt(D * A * RADIUS_SHARE / quad)
    g = grad_hi[...].astype(F32) + grad_lo[...].astype(F32)
    out[...] = ((step * g + last * direction(g)) * scale).reshape(COLS, D)


def per_device(hidden, head, bias, ids, actions, rewards, values, starts, ratio, samples):
    dma = pltpu.SemaphoreType.DMA
    vmem = pltpu.VMEM

    def row(x):
        return x.reshape(1, -1)

    result = pl.pallas_call(
        kernel,
        out_shape=jax.ShapeDtypeStruct((COLS, D), F32),
        in_specs=[pl.BlockSpec(memory_space=pltpu.MemorySpace.HBM)] * 10,
        out_specs=pl.BlockSpec(memory_space=pltpu.VMEM),
        scratch_shapes=[
            vmem((ROWS, D), BF16),
            vmem((D, COLS), BF16),
            vmem((AGENTS, COLS), F32),
            vmem((1, ROWS), jnp.int32),
            vmem((1, ROWS), jnp.int32),
            vmem((1, ROWS), F32),
            vmem((1, ROWS), F32),
            vmem((1, ROWS), jnp.int32),
            vmem((1, ROWS), F32),
            vmem((1, SAMPLES), jnp.int32),
            dma((10,)),
            vmem((COLS, ROWS), F32),
            vmem((COLS, ROWS), BF16),
            vmem((16, 8, D), F32),
            vmem((16, 8, D), BF16),
            vmem((16, 8, D), BF16),
            vmem((16, 8, D), BF16),
            vmem((8, 2, ROWS), F32),
            vmem((8, 1, ROWS), F32),
            vmem((8, 2, ROWS), F32),
            vmem((8, 8, 128), F32),
            vmem((8, 8, 128), F32),
            vmem((8, 8, 128), F32),
            vmem((8, 1, 128), F32),
            vmem((8, 1, 128), F32),
            vmem((8, 1, 128), F32),
            vmem((8, 1, 128), F32),
            vmem((2, NY, 8, LEFT), F32),
            vmem((2, NZ, 2, 8, D - LEFT), F32),
            vmem((NY, 8, LEFT), F32),
            vmem((NZ, 2, 8, D - LEFT), F32),
            vmem((NY, 8, LEFT), F32),
            vmem((NZ, 2, 8, D - LEFT), F32),
            vmem((NY, 8, LEFT), BF16),
            vmem((NZ, 2, 8, D - LEFT), BF16),
            vmem((NY, 8, LEFT), BF16),
            vmem((NZ, 2, 8, D - LEFT), BF16),
            vmem((2, NZ, 8, 384), F32),
            vmem((2, NY, 8, 256), F32),
            vmem((2, NZ, 8, 384), F32),
            vmem((2, NY, 8, 256), F32),
            dma((10, 8)),
            dma((10, 8)),
            dma((2, 6, 8)),
            dma((2, 6, 8)),
            dma((3, 6, 8)),
            dma((3, 6, 8)),
        ],
        compiler_params=pltpu.CompilerParams(
            collective_id=0, has_side_effects=True, vmem_limit_bytes=61 * 1024 * 1024
        ),
        name="step",
    )(
        hidden, head, bias, row(ids), row(actions), row(rewards), row(values), row(starts),
        row(ratio), row(samples),
    )
    return result.T


def solution(mesh):
    placed = (P("dp", None), P(None, "mp"), P(None, "mp")) + (P("dp"),) * 7
    return jax.shard_map(
        per_device, mesh=mesh, in_specs=placed, out_specs=P(None, "mp"), check_vma=False
    )
```

```python
import functools
import math

import jax
import jax.numpy as jnp
from jax import lax
from jax.experimental import pallas as pl
from jax.experimental.pallas import tpu as pltpu
from jax.sharding import PartitionSpec as P

D = 2560
A = 1024
AGENTS = 8
SEQ_LEN = 64
GAMMA = 0.99
TRACE_DECAY = 0.95
DAMPING = 0.001
RADIUS_SHARE = 0.001

MESH = pl.DeviceIdType.MESH
F32 = jnp.float32
BF16 = jnp.bfloat16
NY = 8
NZ = 4
NM = 8
ROWS = 512
SAMPLES = 2048
COLS = 128
LEFT = 1536
FAR_FIRST = (4, 3, 5, 2, 6, 1, 7)
NEAR_FIRST = (1, 7, 2, 6, 3, 5, 4)
CORE_ORDER = (
    ("a", 4), ("b", 3), ("a", 3), ("a", 5), ("b", 1), ("a", 2), ("a", 6), ("b", 2),
    ("a", 1), ("a", 7), ("a", 0), ("b", 0),
)


def kernel(
    hidden_in, head_in, bias_in, ids_in, actions_in, rewards_in, values_in, starts_in, ratio_in, samples_in,
    out,
    hidden, head, bias, ids, actions, rewards, values, starts, ratio, samples, loads,
    probs, logit_grad, part, grad_hi, grad_lo, image_hi,
    peak_box, centre_box, final_box, dots_m, dots_y, dots_q, adv_y, adv_q, curv_y, curv_q,
    core_a, core_b, send_a32, send_b32, y_a32, z_b32, send_a16, send_b16, y_a16, z_b16,
    own_a, own_b, z_a, y_b,
    small_s, small_r, rs_s, rs_r, ag_s, ag_r,
):
    dp, me_m = lax.axis_index("dp"), lax.axis_index("mp")
    core = lax.rem(dp, 2)
    y = lax.rem(dp // 2, NY)
    z = dp // (2 * NY)
    q = z * 2 + core

    def at_y(k):
        return ((z * NY + k) * 2 + core, me_m)

    def at_q(k):
        return ((k // 2 * NY + y) * 2 + lax.rem(k, 2), me_m)

    def at_z(k):
        return ((k * NY + y) * 2 + core, me_m)

    def at_m(k):
        return (dp, k)

    other = (dp + 1 - 2 * core, me_m)

    barrier = pltpu.get_barrier_semaphore()
    for o in range(1, 8):
        for target in (
            at_y(lax.rem(y + o, NY)),
            at_q(lax.rem(q + o, 8)),
            at_m(lax.rem(me_m + o, NM)),
        ):
            pl.semaphore_signal(barrier, inc=1, device_id=target, device_id_type=MESH)

    fetches = [
        pltpu.make_async_copy(src, dst, loads.at[k])
        for k, (src, dst) in enumerate(
            (
                (rewards_in, rewards), (values_in, values), (starts_in, starts),
                (hidden_in, hidden), (head_in, head), (bias_in, bias), (ids_in, ids),
                (actions_in, actions), (ratio_in, ratio), (samples_in, samples),
            )
        )
    ]
    for fetch in fetches:
        fetch.start()

    def copy(src, dst, send, recv, target):
        return pltpu.make_async_remote_copy(
            src_ref=src, dst_ref=dst, send_sem=send, recv_sem=recv,
            device_id=target, device_id_type=MESH,
        )

    def swap_start(n, box, me, place):
        for o in range(1, 8):
            copy(
                box.at[me], box.at[me], small_s.at[n, o], small_r.at[n, me],
                place(lax.rem(me + o, 8)),
            ).start()

    def swap_wait(n, box, me, place):
        for o in range(1, 8):
            k = lax.rem(me + o, 8)
            c = copy(box.at[k], box.at[k], small_s.at[n, o], small_r.at[n, k], place(k))
            c.wait_send()
            c.wait_recv()

    def total(box):
        acc = box[0]
        for k in range(1, 8):
            acc = acc + box[k]
        return acc

    def lane_part(row):
        return row[:, 0:128] + row[:, 128:256] + row[:, 256:384] + row[:, 384:512]

    for fetch in fetches[:3]:
        fetch.wait()

    def ahead(x, s):
        return pltpu.roll(x, ROWS - s, 1)

    def wide(ref):
        return jnp.broadcast_to(ref[...].astype(F32), (8, ROWS))

    position = lax.broadcasted_iota(jnp.int32, (8, ROWS), 1)
    value = wide(values)
    ends = (lax.rem(position, SEQ_LEN) == SEQ_LEN - 1) | (ahead(wide(starts), 1) > 0.5)
    continues = jnp.where(ends, 0.0, 1.0)
    advantage = wide(rewards) + GAMMA * continues * ahead(value, 1) - value
    keeps = GAMMA * TRACE_DECAY * continues
    for s in (1, 2, 4, 8, 16, 32):
        advantage = advantage + keeps * ahead(advantage, s)
        keeps = keeps * ahead(keeps, s)
    advantage = advantage[0:1]
    adv_y[y] = lane_part(advantage)

    for fetch in fetches[3:]:
        fetch.wait()

    logits = jnp.dot(hidden[...], head[...], preferred_element_type=F32).T
    bias_t = bias[...].T
    agent = ids[...]
    for k in range(AGENTS):
        logits = logits + jnp.where(agent == k, bias_t[:, k : k + 1], 0.0)
    peak = jnp.max(logits, axis=0, keepdims=True)
    exponent = jnp.exp(logits - peak)
    peak_box[me_m, 0:1] = peak
    peak_box[me_m, 1:2] = jnp.sum(exponent, axis=0, keepdims=True)
    probs[...] = exponent
    pl.semaphore_wait(barrier, 21)
    swap_start(0, adv_y, y, at_y)
    swap_start(1, peak_box, me_m, at_m)

    local = samples[...] - dp * ROWS
    high = lax.shift_right_logical(local, 7)
    low = lax.bitwise_and(local, 127)
    high_hot = (lax.broadcasted_iota(jnp.int32, (8, SAMPLES), 0) == high).astype(F32).astype(BF16)
    low_hot = (lax.broadcasted_iota(jnp.int32, (128, SAMPLES), 0) == low).astype(F32).astype(BF16)
    tally = lax.dot_general(
        high_hot, low_hot, (((1,), (1,)), ((), ())), preferred_element_type=F32
    )
    count = jnp.concatenate([tally[0:1], tally[1:2], tally[2:3], tally[3:4]], axis=1)

    swap_wait(0, adv_y, y, at_y)
    adv_q[q] = total(adv_y)
    swap_start(2, adv_q, q, at_q)

    swap_wait(1, peak_box, me_m, at_m)
    row_peak = peak_box[0, 0:1]
    for k in range(1, NM):
        row_peak = jnp.maximum(row_peak, peak_box[k, 0:1])
    denominator = peak_box[0, 1:2] * jnp.exp(peak_box[0, 0:1] - row_peak)
    for k in range(1, NM):
        denominator = denominator + peak_box[k, 1:2] * jnp.exp(peak_box[k, 0:1] - row_peak)
    prob = probs[...] * (jnp.exp(peak - row_peak) / denominator)
    probs[...] = prob

    swap_wait(2, adv_q, q, at_q)
    tokens = ROWS * 64
    adv_mean = jnp.sum(total(adv_q), axis=1, keepdims=True) / tokens
    weight = ratio[...] * (advantage - adv_mean) / tokens
    picked = lax.broadcasted_iota(jnp.int32, (COLS, ROWS), 0) == actions[...] - me_m * COLS
    logit_grad[...] = (weight * (jnp.where(picked, 1.0, 0.0) - prob)).astype(BF16)

    def project():
        for j in range(5):
            cols = slice(512 * j, 512 * (j + 1))
            part[:, :, cols] = jnp.dot(
                logit_grad[...], hidden[:, cols], preferred_element_type=F32
            ).reshape(16, 8, 512)

    def scatter(n, send_a, send_b, y_a, z_b):
        def core_copy(kind, o):
            if kind == "a":
                k = (1 - core) * 8 + lax.rem(y + o, NY)
                return copy(
                    part.at[k, :, 0:LEFT], core_a.at[n, o], rs_s.at[n, 0, o], rs_r.at[n, 0, o], other
                )
            k = (1 - core) * 8 + lax.rem(z + o, NZ) * 2
            return copy(
                part.at[pl.ds(k, 2), :, LEFT:D], core_b.at[n, o],
                rs_s.at[n, 1, o], rs_r.at[n, 1, o], other,
            )

        def leg_a(o, k):
            return copy(send_a.at[o], y_a.at[o], rs_s.at[n, 2, o], rs_r.at[n, 2, o], at_y(k))

        def leg_b(o, k):
            return copy(send_b.at[o], z_b.at[o], rs_s.at[n, 3, o], rs_r.at[n, 3, o], at_z(k))

        sends = []
        for kind, o in CORE_ORDER:
            c = core_copy(kind, o)
            c.start()
            sends.append(c)
        for kind, o in CORE_ORDER:
            core_copy(kind, o).wait_recv()
            if kind == "a":
                k = lax.rem(y + o, NY)
                term = part[core * 8 + k, :, 0:LEFT] + core_a[n, o]
                if o == 0:
                    acc_a = term
                    continue
                send_a[o] = term.astype(send_a.dtype)
                c = leg_a(o, k)
            else:
                k = lax.rem(z + o, NZ)
                term = part[pl.ds(core * 8 + 2 * k, 2), :, LEFT:D] + core_b[n, o]
                if o == 0:
                    acc_b = term
                    continue
                send_b[o] = term.astype(send_b.dtype)
                c = leg_b(o, k)
            c.start()
            sends.append(c)
        for o in (1, 2, 3):
            leg_b(o, lax.rem(z + NZ - o, NZ)).wait_recv()
            acc_b = acc_b + z_b[o].astype(F32)
        for k in range(NY):
            own_b[n, k] = acc_b[k // 4, :, 256 * (k % 4) : 256 * (k % 4 + 1)]
        for o in FAR_FIRST:
            k = lax.rem(y + o, NY)
            c = copy(own_b.at[n, k], y_b.at[n, o], rs_s.at[n, 4, o], rs_r.at[n, 4, o], at_y(k))
            c.start()
            sends.append(c)
        for o in NEAR_FIRST:
            leg_a(o, lax.rem(y + NY - o, NY)).wait_recv()
            acc_a = acc_a + y_a[o].astype(F32)
        for k in range(NZ):
            own_a[n, k] = acc_a[:, 384 * k : 384 * (k + 1)]
        for o in (3, 2, 1):
            k = lax.rem(z + o, NZ)
            c = copy(own_a.at[n, k], z_a.at[n, o], rs_s.at[n, 5, o], rs_r.at[n, 5, o], at_z(k))
            c.start()
            sends.append(c)
        shard_b = own_b[n, y]
        for o in NEAR_FIRST:
            k = lax.rem(y + NY - o, NY)
            copy(
                own_b.at[n, k], y_b.at[n, o], rs_s.at[n, 4, o], rs_r.at[n, 4, o], at_y(k)
            ).wait_recv()
            shard_b = shard_b + y_b[n, o]
        shard_a = own_a[n, z]
        for o in (1, 2, 3):
            k = lax.rem(z + NZ - o, NZ)
            copy(
                own_a.at[n, k], z_a.at[n, o], rs_s.at[n, 5, o], rs_r.at[n, 5, o], at_z(k)
            ).wait_recv()
            shard_a = shard_a + z_a[n, o]
        for c in sends:
            c.wait_send()
        return shard_a, shard_b

    def spot_a(full, ky, kz):
        return full.at[core * 8 + ky, :, pl.ds(pl.multiple_of(kz * 384, 128), 384)]

    def spot_b(full, ky, kz):
        columns = pl.ds(pl.multiple_of(LEFT + lax.rem(ky, 4) * 256, 128), 256)
        return full.at[core * 8 + 2 * kz + ky // 4, :, columns]

    def line_a(full, kc, ky):
        return full.at[kc * 8 + ky, :, 0:LEFT]

    def line_b(full, kc, kz):
        return full.at[pl.ds(kc * 8 + 2 * kz, 2), :, LEFT:D]

    def gather_start(n, full):
        sends = []

        def begin(ref, kind, o, target):
            c = copy(ref, ref, ag_s.at[n, kind, o], ag_r.at[n, kind, o], target)
            c.start()
            sends.append(c)

        for o in (3, 2, 1):
            begin(spot_a(full, y, z), 0, o, at_z(lax.rem(z + o, NZ)))
        for o in FAR_FIRST:
            begin(spot_b(full, y, z), 1, o, at_y(lax.rem(y + o, NY)))
        for o in (1, 2, 3):
            k = lax.rem(z + NZ - o, NZ)
            there = spot_a(full, y, k)
            copy(there, there, ag_s.at[n, 0, o], ag_r.at[n, 0, o], at_z(k)).wait_recv()
        for o in FAR_FIRST:
            begin(line_a(full, core, y), 2, o, at_y(lax.rem(y + o, NY)))
        begin(line_a(full, core, y), 4, 0, other)
        for o in NEAR_FIRST:
            k = lax.rem(y + NY - o, NY)
            there = spot_b(full, k, z)
            copy(there, there, ag_s.at[n, 1, o], ag_r.at[n, 1, o], at_y(k)).wait_recv()
        for o in (3, 2, 1):
            begin(line_b(full, core, z), 3, o, at_z(lax.rem(z + o, NZ)))
        begin(line_b(full, core, z), 5, 0, other)
        return sends

    def gather_wait(n, full, sends):
        def arrive(ref, kind, o, source, onward):
            copy(ref, ref, ag_s.at[n, kind, o], ag_r.at[n, kind, o], source).wait_recv()
            if onward:
                c = copy(ref, ref, ag_s.at[n, onward, o], ag_r.at[n, onward, o], other)
                c.start()
                sends.append(c)

        for kind, o in (("a", 1), ("a", 7), ("b", 1), ("a", 2), ("a", 6), ("b", 2), ("b", 3), ("a", 3), ("a", 5), ("a", 4)):
            if kind == "a":
                k = lax.rem(y + NY - o, NY)
                arrive(line_a(full, core, k), 2, o, at_y(k), 4)
            else:
                k = lax.rem(z + NZ - o, NZ)
                arrive(line_b(full, core, k), 3, o, at_z(k), 5)
        for o in range(NY):
            arrive(line_a(full, 1 - core, lax.rem(y + NY - o, NY)), 4, o, other, 0)
        for o in range(NZ):
            arrive(line_b(full, 1 - core, lax.rem(z + NZ - o, NZ)), 5, o, other, 0)
        for c in sends:
            c.wait_send()

    def keep(full, shards):
        shard_a, shard_b = shards
        full[core * 8 + y, :, pl.ds(pl.multiple_of(z * 384, 128), 384)] = shard_a.astype(BF16)
        columns = pl.ds(pl.multiple_of(LEFT + lax.rem(y, 4) * 256, 128), 256)
        full[core * 8 + 2 * z + y // 4, :, columns] = shard_b.astype(BF16)

    def lift(vector):
        return lax.dot_general(
            vector.reshape(COLS, D).astype(BF16), hidden[...], (((1,), (1,)), ((), ())),
            preferred_element_type=F32,
        )

    project()
    grad_piece = scatter(0, send_a32, send_b32, y_a32, z_b32)
    keep(grad_hi, grad_piece)
    keep(grad_lo, [x - x.astype(BF16).astype(F32) for x in grad_piece])
    gather_wait(0, grad_hi, gather_start(0, grad_hi))

    lifted = lift(grad_hi[...].astype(F32))
    prob = probs[...]
    centre_box[me_m] = jnp.sum(prob * lifted, axis=0, keepdims=True)
    swap_start(3, centre_box, me_m, at_m)
    swap_wait(3, centre_box, me_m, at_m)
    logit_grad[...] = (count * (prob * (lifted - total(centre_box)))).astype(BF16)
    project()
    fisher = [x / (SAMPLES * 64) for x in scatter(1, send_a16, send_b16, y_a16, z_b16)]
    keep(image_hi, fisher)
    image_piece = [f + DAMPING * g for f, g in zip(fisher, grad_piece)]
    def folded(left, right):
        terms = [
            l[:, k : k + 128] * r[:, k : k + 128]
            for l, r in zip(left, right)
            for k in range(0, l.shape[1], 128)
        ]
        return jnp.sum(sum(terms[1:], terms[0]), axis=0, keepdims=True)

    dots_m[me_m, 0:1] = folded(grad_piece, grad_piece)
    dots_m[me_m, 1:2] = folded(grad_piece, image_piece)
    dots_m[me_m, 2:3] = folded(image_piece, image_piece)
    dots_m[me_m, 3:8] = jnp.zeros((5, 128), F32)
    swap_start(4, dots_m, me_m, at_m)
    sends = gather_start(1, image_hi)
    swap_wait(4, dots_m, me_m, at_m)
    dots_y[y] = total(dots_m)
    swap_start(5, dots_y, y, at_y)
    swap_wait(5, dots_y, y, at_y)
    dots_q[q] = total(dots_y)
    swap_start(6, dots_q, q, at_q)
    gather_wait(1, image_hi, sends)
    swap_wait(6, dots_q, q, at_q)
    dots = jnp.sum(total(dots_q), axis=1, keepdims=True)
    rr, curvature, image_sq = dots[0:1], dots[1:2], dots[2:3]
    step = rr / curvature
    rr_next = rr - 2.0 * step * curvature + step * step * image_sq
    beta = rr_next / rr
    quad = step * step * curvature

    def direction(g):
        return g - step * (image_hi[...].astype(F32) + DAMPING * g) + beta * g

    lifted = lift(direction(grad_hi[...].astype(F32)))
    prob = probs[...]
    mass = jnp.sum(prob, axis=0, keepdims=True)
    moment = jnp.sum(prob * lifted, axis=0, keepdims=True)
    mean = jnp.where(mass > 0.0, moment / jnp.where(mass > 0.0, mass, 1.0), 0.0)
    spread = lifted - mean
    final_box[me_m, 0:1] = moment
    final_box[me_m, 1:2] = jnp.sum(prob * spread * spread, axis=0, keepdims=True)
    swap_start(7, final_box, me_m, at_m)
    sends = gather_start(2, grad_lo)
    swap_wait(7, final_box, me_m, at_m)
    sums = total(final_box)
    centre, variance = sums[0:1], sums[1:2]
    for k in range(NM):
        mass = peak_box[k, 1:2] * (jnp.exp(peak_box[k, 0:1] - row_peak) / denominator)
        mean = jnp.where(mass > 0.0, final_box[k, 0:1] / jnp.where(mass > 0.0, mass, 1.0), 0.0)
        variance = variance + mass * (mean - centre) * (mean - centre)
    curv_y[y] = lane_part(count * variance)
    swap_start(8, curv_y, y, at_y)
    swap_wait(8, curv_y, y, at_y)
    curv_q[q] = total(curv_y)
    swap_start(9, curv_q, q, at_q)
    gather_wait(2, grad_lo, sends)
    swap_wait(9, curv_q, q, at_q)
    curvature = jnp.sum(total(curv_q), axis=1, keepdims=True) / (SAMPLES * 64)
    curvature = curvature + DAMPING * (rr_next + beta * beta * rr)
    last = rr_next / curvature
    quad = quad + last * last * curvature
    scale = jnp.sqrt(D * A * RADIUS_SHARE / quad)
    g = grad_hi[...].astype(F32) + grad_lo[...].astype(F32)
    out[...] = ((step * g + last * direction(g)) * scale).reshape(COLS, D)


def per_device(hidden, head, bias, ids, actions, rewards, values, starts, ratio, samples):
    dma = pltpu.SemaphoreType.DMA
    vmem = pltpu.VMEM

    def row(x):
        return x.reshape(1, -1)

    result = pl.pallas_call(
        kernel,
        out_shape=jax.ShapeDtypeStruct((COLS, D), F32),
        in_specs=[pl.BlockSpec(memory_space=pltpu.MemorySpace.HBM)] * 10,
        out_specs=pl.BlockSpec(memory_space=pltpu.VMEM),
        scratch_shapes=[
            vmem((ROWS, D), BF16),
            vmem((D, COLS), BF16),
            vmem((AGENTS, COLS), F32),
            vmem((1, ROWS), jnp.int32),
            vmem((1, ROWS), jnp.int32),
            vmem((1, ROWS), F32),
            vmem((1, ROWS), F32),
            vmem((1, ROWS), jnp.int32),
            vmem((1, ROWS), F32),
            vmem((1, SAMPLES), jnp.int32),
            dma((10,)),
            vmem((COLS, ROWS), F32),
            vmem((COLS, ROWS), BF16),
            vmem((16, 8, D), F32),
            vmem((16, 8, D), BF16),
            vmem((16, 8, D), BF16),
            vmem((16, 8, D), BF16),
            vmem((8, 2, ROWS), F32),
            vmem((8, 1, ROWS), F32),
            vmem((8, 2, ROWS), F32),
            vmem((8, 8, 128), F32),
            vmem((8, 8, 128), F32),
            vmem((8, 8, 128), F32),
            vmem((8, 1, 128), F32),
            vmem((8, 1, 128), F32),
            vmem((8, 1, 128), F32),
            vmem((8, 1, 128), F32),
            vmem((2, NY, 8, LEFT), F32),
            vmem((2, NZ, 2, 8, D - LEFT), F32),
            vmem((NY, 8, LEFT), F32),
            vmem((NZ, 2, 8, D - LEFT), F32),
            vmem((NY, 8, LEFT), F32),
            vmem((NZ, 2, 8, D - LEFT), F32),
            vmem((NY, 8, LEFT), BF16),
            vmem((NZ, 2, 8, D - LEFT), BF16),
            vmem((NY, 8, LEFT), BF16),
            vmem((NZ, 2, 8, D - LEFT), BF16),
            vmem((2, NZ, 8, 384), F32),
            vmem((2, NY, 8, 256), F32),
            vmem((2, NZ, 8, 384), F32),
            vmem((2, NY, 8, 256), F32),
            dma((10, 8)),
            dma((10, 8)),
            dma((2, 6, 8)),
            dma((2, 6, 8)),
            dma((3, 6, 8)),
            dma((3, 6, 8)),
        ],
        compiler_params=pltpu.CompilerParams(
            collective_id=0, has_side_effects=True, vmem_limit_bytes=40 * 1024 * 1024
        ),
        name="step",
    )(
        *(
            pltpu.with_memory_space_constraint(x, pltpu.MemorySpace.HBM)
            for x in (
                hidden, head, bias, row(ids), row(actions), row(rewards), row(values), row(starts),
                row(ratio), row(samples),
            )
        )
    )
    return result.T


def solution(mesh):
    placed = (P("dp", None), P(None, "mp"), P(None, "mp")) + (P("dp"),) * 7
    return jax.shard_map(
        per_device, mesh=mesh, in_specs=placed, out_specs=P(None, "mp"), check_vma=False
    )
```

```python
import functools
import math

import jax
import jax.numpy as jnp
from jax import lax
from jax.experimental import pallas as pl
from jax.experimental.pallas import tpu as pltpu
from jax.sharding import PartitionSpec as P

D = 2560
A = 1024
AGENTS = 8
SEQ_LEN = 64
GAMMA = 0.99
TRACE_DECAY = 0.95
DAMPING = 0.001
RADIUS_SHARE = 0.001

MESH = pl.DeviceIdType.MESH
F32 = jnp.float32
BF16 = jnp.bfloat16
NY = 8
NZ = 4
NM = 8
ROWS = 512
SAMPLES = 2048
COLS = 128
LEFT = 1536
FAR_FIRST = (4, 3, 5, 2, 6, 1, 7)
NEAR_FIRST = (1, 7, 2, 6, 3, 5, 4)
ARRIVALS = (
    ("a", 1), ("a", 7), ("b", 1), ("a", 2), ("a", 6), ("b", 2), ("b", 3), ("a", 3), ("a", 5),
    ("a", 4),
)
CORE_ORDER = (
    ("a", 4), ("b", 3), ("a", 3), ("a", 5), ("b", 1), ("a", 2), ("a", 6), ("b", 2),
    ("a", 1), ("a", 7), ("a", 0), ("b", 0),
)


def kernel(
    hidden_in, head_in, bias_in, ids_in, actions_in, rewards_in, values_in, starts_in, ratio_in, samples_in,
    out,
    hidden, head, bias, ids, actions, rewards, values, starts, ratio, samples, loads,
    probs, lifted_grad, logit_grad, part, grad_hi, grad_lo, resid_hi,
    peak_box, centre_box, final_box, first_y, first_q, dots_m, dots_y, dots_q, adv_y, adv_q, curv_y, curv_q,
    core_a, core_b, send_a32, send_b32, y_a32, z_b32, send_a16, send_b16, y_a16, z_b16,
    own_a, own_b, z_a, y_b,
    small_s, small_r, rs_s, rs_r, rs_core, ag_s, ag_r, ag_line,
):
    dp, me_m = lax.axis_index("dp"), lax.axis_index("mp")
    core = lax.rem(dp, 2)
    y = lax.rem(dp // 2, NY)
    z = dp // (2 * NY)
    q = z * 2 + core

    def at_y(k):
        return ((z * NY + k) * 2 + core, me_m)

    def at_q(k):
        return ((k // 2 * NY + y) * 2 + lax.rem(k, 2), me_m)

    def at_z(k):
        return ((k * NY + y) * 2 + core, me_m)

    def at_m(k):
        return (dp, k)

    other = (dp + 1 - 2 * core, me_m)

    barrier = pltpu.get_barrier_semaphore()
    for o in range(1, 8):
        for target in (
            at_y(lax.rem(y + o, NY)),
            at_q(lax.rem(q + o, 8)),
            at_m(lax.rem(me_m + o, NM)),
        ):
            pl.semaphore_signal(barrier, inc=1, device_id=target, device_id_type=MESH)

    fetches = [
        pltpu.make_async_copy(src, dst, loads.at[k])
        for k, (src, dst) in enumerate(
            (
                (rewards_in, rewards), (values_in, values), (starts_in, starts),
                (hidden_in, hidden), (head_in, head), (bias_in, bias), (ids_in, ids),
                (actions_in, actions), (ratio_in, ratio), (samples_in, samples),
            )
        )
    ]
    for fetch in fetches:
        fetch.start()

    def copy(src, dst, send, recv, target):
        return pltpu.make_async_remote_copy(
            src_ref=src, dst_ref=dst, send_sem=send, recv_sem=recv,
            device_id=target, device_id_type=MESH,
        )

    def wait_sent(view, sem):
        copy(view, view, sem, sem, other).wait_send()

    def wait_come(view, sem):
        copy(view, view, sem, sem, other).wait_recv()

    def swap_start(n, box, me, place):
        for o in range(1, 8):
            copy(
                box.at[me], box.at[me], small_s.at[n], small_r.at[n], place(lax.rem(me + o, 8))
            ).start()

    def swap_wait(n, box, me, place):
        wait_come(box.at[0:7], small_r.at[n])
        wait_sent(box.at[0:7], small_s.at[n])

    def total(box):
        acc = box[0]
        for k in range(1, 8):
            acc = acc + box[k]
        return acc

    def lane_part(row):
        return row[:, 0:128] + row[:, 128:256] + row[:, 256:384] + row[:, 384:512]

    for fetch in fetches[:3]:
        fetch.wait()

    def ahead(x, s):
        return pltpu.roll(x, ROWS - s, 1)

    def wide(ref):
        return jnp.broadcast_to(ref[...].astype(F32), (8, ROWS))

    position = lax.broadcasted_iota(jnp.int32, (8, ROWS), 1)
    value = wide(values)
    ends = (lax.rem(position, SEQ_LEN) == SEQ_LEN - 1) | (ahead(wide(starts), 1) > 0.5)
    continues = jnp.where(ends, 0.0, 1.0)
    advantage = wide(rewards) + GAMMA * continues * ahead(value, 1) - value
    keeps = GAMMA * TRACE_DECAY * continues
    for s in (1, 2, 4, 8, 16, 32):
        advantage = advantage + keeps * ahead(advantage, s)
        keeps = keeps * ahead(keeps, s)
    advantage = advantage[0:1]
    adv_y[y] = lane_part(advantage)

    for fetch in fetches[3:]:
        fetch.wait()

    logits = jnp.dot(hidden[...], head[...], preferred_element_type=F32).T
    bias_t = bias[...].T
    agent = ids[...]
    for k in range(AGENTS):
        logits = logits + jnp.where(agent == k, bias_t[:, k : k + 1], 0.0)
    peak = jnp.max(logits, axis=0, keepdims=True)
    exponent = jnp.exp(logits - peak)
    peak_box[me_m, 0:1] = peak
    peak_box[me_m, 1:2] = jnp.sum(exponent, axis=0, keepdims=True)
    probs[...] = exponent
    pl.semaphore_wait(barrier, 21)
    swap_start(0, adv_y, y, at_y)
    swap_start(1, peak_box, me_m, at_m)

    local = samples[...] - dp * ROWS
    high = lax.shift_right_logical(local, 7)
    low = lax.bitwise_and(local, 127)
    high_hot = (lax.broadcasted_iota(jnp.int32, (8, SAMPLES), 0) == high).astype(F32).astype(BF16)
    low_hot = (lax.broadcasted_iota(jnp.int32, (128, SAMPLES), 0) == low).astype(F32).astype(BF16)
    tally = lax.dot_general(
        high_hot, low_hot, (((1,), (1,)), ((), ())), preferred_element_type=F32
    )
    count = jnp.concatenate([tally[0:1], tally[1:2], tally[2:3], tally[3:4]], axis=1)

    swap_wait(0, adv_y, y, at_y)
    adv_q[q] = total(adv_y)
    swap_start(2, adv_q, q, at_q)

    swap_wait(1, peak_box, me_m, at_m)
    row_peak = peak_box[0, 0:1]
    for k in range(1, NM):
        row_peak = jnp.maximum(row_peak, peak_box[k, 0:1])
    denominator = peak_box[0, 1:2] * jnp.exp(peak_box[0, 0:1] - row_peak)
    for k in range(1, NM):
        denominator = denominator + peak_box[k, 1:2] * jnp.exp(peak_box[k, 0:1] - row_peak)
    prob = probs[...] * (jnp.exp(peak - row_peak) / denominator)
    probs[...] = prob

    swap_wait(2, adv_q, q, at_q)
    tokens = ROWS * 64
    adv_mean = jnp.sum(total(adv_q), axis=1, keepdims=True) / tokens
    weight = ratio[...] * (advantage - adv_mean) / tokens
    picked = lax.broadcasted_iota(jnp.int32, (COLS, ROWS), 0) == actions[...] - me_m * COLS
    logit_grad[...] = (weight * (jnp.where(picked, 1.0, 0.0) - prob)).astype(BF16)

    def project():
        for j in range(5):
            cols = slice(512 * j, 512 * (j + 1))
            part[:, :, cols] = jnp.dot(
                logit_grad[...], hidden[:, cols], preferred_element_type=F32
            ).reshape(16, 8, 512)

    def scatter(n, send_a, send_b, y_a, z_b, between):
        def core_copy(kind, o):
            if kind == "a":
                k = (1 - core) * 8 + lax.rem(y + o, NY)
                return copy(
                    part.at[k, :, 0:LEFT], core_a.at[n, o], rs_s.at[n, 0], rs_core.at[n, o], other
                )
            k = (1 - core) * 8 + lax.rem(z + o, NZ) * 2
            return copy(
                part.at[pl.ds(k, 2), :, LEFT:D], core_b.at[n, o],
                rs_s.at[n, 1], rs_core.at[n, 8 + o], other,
            )

        for kind, o in CORE_ORDER:
            core_copy(kind, o).start()
        for kind, o in CORE_ORDER:
            core_copy(kind, o).wait_recv()
            if kind == "a":
                k = lax.rem(y + o, NY)
                term = part[core * 8 + k, :, 0:LEFT] + core_a[n, o]
                if o == 0:
                    acc_a = term
                    continue
                send_a[o] = term.astype(send_a.dtype)
                copy(send_a.at[o], y_a.at[o], rs_s.at[n, 2], rs_r.at[n, 2], at_y(k)).start()
            else:
                k = lax.rem(z + o, NZ)
                term = part[pl.ds(core * 8 + 2 * k, 2), :, LEFT:D] + core_b[n, o]
                if o == 0:
                    acc_b = term
                    continue
                send_b[o] = term.astype(send_b.dtype)
                copy(send_b.at[o], z_b.at[o], rs_s.at[n, 3], rs_r.at[n, 3], at_z(k)).start()
        wait_come(z_b.at[1:4], rs_r.at[n, 3])
        for o in (1, 2, 3):
            acc_b = acc_b + z_b[o].astype(F32)
        for k in range(NY):
            own_b[n, k] = acc_b[k // 4, :, 256 * (k % 4) : 256 * (k % 4 + 1)]
        for o in FAR_FIRST:
            k = lax.rem(y + o, NY)
            copy(own_b.at[n, k], y_b.at[n, o], rs_s.at[n, 4], rs_r.at[n, 4], at_y(k)).start()
        between()
        wait_come(y_a.at[1:8], rs_r.at[n, 2])
        for o in NEAR_FIRST:
            acc_a = acc_a + y_a[o].astype(F32)
        for k in range(NZ):
            own_a[n, k] = acc_a[:, 384 * k : 384 * (k + 1)]
        for o in (3, 2, 1):
            k = lax.rem(z + o, NZ)
            copy(own_a.at[n, k], z_a.at[n, o], rs_s.at[n, 5], rs_r.at[n, 5], at_z(k)).start()
        shard_b = own_b[n, y]
        wait_come(y_b.at[n, 1:8], rs_r.at[n, 4])
        for o in NEAR_FIRST:
            shard_b = shard_b + y_b[n, o]
        shard_a = own_a[n, z]
        wait_come(z_a.at[n, 1:4], rs_r.at[n, 5])
        for o in (1, 2, 3):
            shard_a = shard_a + z_a[n, o]
        return shard_a, shard_b

    def scatter_end(n, send_a, send_b):
        wait_sent(part.at[0:8, :, 0:LEFT], rs_s.at[n, 0])
        wait_sent(part.at[0:8, :, LEFT:D], rs_s.at[n, 1])
        wait_sent(send_a.at[1:8], rs_s.at[n, 2])
        wait_sent(send_b.at[1:4], rs_s.at[n, 3])
        wait_sent(own_b.at[n, 1:8], rs_s.at[n, 4])
        wait_sent(own_a.at[n, 1:4], rs_s.at[n, 5])

    def spot_a(full, ky, kz):
        return full.at[core * 8 + ky, :, pl.ds(pl.multiple_of(kz * 384, 128), 384)]

    def spot_b(full, ky, kz):
        columns = pl.ds(pl.multiple_of(LEFT + lax.rem(ky, 4) * 256, 128), 256)
        return full.at[core * 8 + 2 * kz + ky // 4, :, columns]

    def line_a(full, kc, ky):
        return full.at[kc * 8 + ky, :, 0:LEFT]

    def line_b(full, kc, kz):
        return full.at[pl.ds(kc * 8 + 2 * kz, 2), :, LEFT:D]

    def gather_start(n, full):
        def begin(ref, kind, recv, target):
            copy(ref, ref, ag_s.at[n, kind], recv, target).start()

        mine = core * 8 + y
        for o in (3, 2, 1):
            begin(spot_a(full, y, z), 0, ag_r.at[n, 0], at_z(lax.rem(z + o, NZ)))
        for o in FAR_FIRST:
            begin(spot_b(full, y, z), 1, ag_r.at[n, 1], at_y(lax.rem(y + o, NY)))
        wait_come(full.at[mine, :, 0 : 3 * 384], ag_r.at[n, 0])
        for o in FAR_FIRST:
            begin(line_a(full, core, y), 2, ag_line.at[n, o], at_y(lax.rem(y + o, NY)))
        begin(line_a(full, core, y), 4, ag_r.at[n, 2], other)
        wait_come(full.at[mine, :, 0 : 7 * 256], ag_r.at[n, 1])
        for o in (3, 2, 1):
            begin(line_b(full, core, z), 3, ag_line.at[n, 7 + o], at_z(lax.rem(z + o, NZ)))
        begin(line_b(full, core, z), 5, ag_r.at[n, 3], other)

    def gather_wait(n, full):
        def arrive(ref, line, kind, recv):
            wait_come(ref, ag_line.at[n, line])
            copy(ref, ref, ag_s.at[n, kind], recv, other).start()

        for kind, o in ARRIVALS:
            if kind == "a":
                arrive(line_a(full, core, lax.rem(y + NY - o, NY)), o, 4, ag_r.at[n, 2])
            else:
                arrive(line_b(full, core, lax.rem(z + NZ - o, NZ)), 7 + o, 5, ag_r.at[n, 3])
        wait_come(full.at[pl.ds((1 - core) * 8, 8), :, 0:LEFT], ag_r.at[n, 2])
        wait_come(full.at[pl.ds((1 - core) * 8, 8), :, LEFT:D], ag_r.at[n, 3])

    def gather_end(n, full):
        wait_sent(full.at[0, :, 0 : 3 * 384], ag_s.at[n, 0])
        wait_sent(full.at[0, :, 0 : 7 * 256], ag_s.at[n, 1])
        wait_sent(full.at[0:7, :, 0:LEFT], ag_s.at[n, 2])
        wait_sent(full.at[0:6, :, LEFT:D], ag_s.at[n, 3])
        wait_sent(full.at[0:8, :, 0:LEFT], ag_s.at[n, 4])
        wait_sent(full.at[0:8, :, LEFT:D], ag_s.at[n, 5])

    def keep(full, shards):
        shard_a, shard_b = shards
        full[core * 8 + y, :, pl.ds(pl.multiple_of(z * 384, 128), 384)] = shard_a.astype(BF16)
        columns = pl.ds(pl.multiple_of(LEFT + lax.rem(y, 4) * 256, 128), 256)
        full[core * 8 + 2 * z + y // 4, :, columns] = shard_b.astype(BF16)

    def lift(vector):
        return lax.dot_general(
            vector.reshape(COLS, D).astype(BF16), hidden[...], (((1,), (1,)), ((), ())),
            preferred_element_type=F32,
        )

    def folded(left, right):
        terms = [
            l[:, k : k + 128] * r[:, k : k + 128]
            for l, r in zip(left, right)
            for k in range(0, l.shape[1], 128)
        ]
        return jnp.sum(sum(terms[1:], terms[0]), axis=0, keepdims=True)

    project()
    grad_piece = scatter(0, send_a32, send_b32, y_a32, z_b32, lambda: None)
    keep(grad_hi, grad_piece)
    keep(grad_lo, [x - x.astype(BF16).astype(F32) for x in grad_piece])
    gather_start(0, grad_hi)
    gather_wait(0, grad_hi)
    scatter_end(0, send_a32, send_b32)

    def local_moments(box, prob, lifted):
        mass = jnp.sum(prob, axis=0, keepdims=True)
        moment = jnp.sum(prob * lifted, axis=0, keepdims=True)
        spread = lifted - share(moment, mass)
        box[me_m, 0:1] = moment
        box[me_m, 1:2] = jnp.sum(prob * spread * spread, axis=0, keepdims=True)

    def share(moment, mass):
        return jnp.where(mass > 0.0, moment / jnp.where(mass > 0.0, mass, 1.0), 0.0)

    def row_variance(box, centre):
        variance = jnp.zeros_like(centre)
        for k in range(NM):
            mass = peak_box[k, 1:2] * (jnp.exp(peak_box[k, 0:1] - row_peak) / denominator)
            away = share(box[k, 0:1], mass) - centre
            variance = variance + box[k, 1:2] + mass * away * away
        return variance

    lifted = lift(grad_hi[...].astype(F32))
    lifted_grad[...] = lifted
    prob = probs[...]
    local_moments(centre_box, prob, lifted)
    centre_box[me_m, 2:3] = jnp.concatenate(
        [folded(grad_piece, grad_piece), jnp.zeros((1, ROWS - 128), F32)], axis=1
    )
    swap_start(3, centre_box, me_m, at_m)
    swap_wait(3, centre_box, me_m, at_m)
    centre = total(centre_box)[0:1]
    logit_grad[...] = (count * (prob * (lifted - centre))).astype(BF16)
    first_y[y, 0:1] = lane_part(count * row_variance(centre_box, centre))
    first_y[y, 1:2] = total(centre_box)[2:3, 0:128]
    swap_start(4, first_y, y, at_y)
    project()

    def pass_on():
        swap_wait(4, first_y, y, at_y)
        first_q[q] = total(first_y)
        swap_start(5, first_q, q, at_q)

    summed = scatter(1, send_a16, send_b16, y_a16, z_b16, pass_on)
    swap_wait(5, first_q, q, at_q)
    dots = jnp.sum(total(first_q), axis=1, keepdims=True)
    rr = dots[1:2]
    curvature = dots[0:1] / (SAMPLES * 64) + DAMPING * rr
    step = rr / curvature
    quad = step * step * curvature
    resid_piece = [
        g - step * (f / (SAMPLES * 64) + DAMPING * g) for f, g in zip(summed, grad_piece)
    ]
    keep(resid_hi, resid_piece)
    dots_m[me_m] = folded(resid_piece, resid_piece)
    swap_start(6, dots_m, me_m, at_m)
    gather_start(1, resid_hi)
    swap_wait(6, dots_m, me_m, at_m)
    dots_y[y] = total(dots_m)
    swap_start(7, dots_y, y, at_y)
    swap_wait(7, dots_y, y, at_y)
    dots_q[q] = total(dots_y)
    swap_start(8, dots_q, q, at_q)
    gather_wait(1, resid_hi)

    lifted = lift(resid_hi[...].astype(F32))
    swap_wait(8, dots_q, q, at_q)
    rr_next = jnp.sum(total(dots_q), axis=1, keepdims=True)
    beta = rr_next / rr
    local_moments(final_box, probs[...], lifted + beta * lifted_grad[...])
    swap_start(9, final_box, me_m, at_m)
    gather_start(2, grad_lo)
    swap_wait(9, final_box, me_m, at_m)
    curv_y[y] = lane_part(count * row_variance(final_box, total(final_box)[0:1]))
    swap_start(10, curv_y, y, at_y)
    swap_wait(10, curv_y, y, at_y)
    curv_q[q] = total(curv_y)
    swap_start(11, curv_q, q, at_q)
    gather_wait(2, grad_lo)
    scatter_end(1, send_a16, send_b16)
    for n, full in enumerate((grad_hi, resid_hi, grad_lo)):
        gather_end(n, full)
    swap_wait(11, curv_q, q, at_q)
    curvature = jnp.sum(total(curv_q), axis=1, keepdims=True) / (SAMPLES * 64)
    curvature = curvature + DAMPING * (rr_next + beta * beta * rr)
    last = rr_next / curvature
    quad = quad + last * last * curvature
    scale = jnp.sqrt(D * A * RADIUS_SHARE / quad)
    of_grad = (step + last * beta) * scale
    of_resid = last * scale
    g = grad_hi[...].astype(F32) + grad_lo[...].astype(F32)
    out[...] = (of_grad * g + of_resid * resid_hi[...].astype(F32)).reshape(COLS, D)


def per_device(hidden, head, bias, ids, actions, rewards, values, starts, ratio, samples):
    dma = pltpu.SemaphoreType.DMA
    vmem = pltpu.VMEM

    def row(x):
        return x.reshape(1, -1)

    result = pl.pallas_call(
        kernel,
        out_shape=jax.ShapeDtypeStruct((COLS, D), F32),
        in_specs=[pl.BlockSpec(memory_space=pltpu.MemorySpace.HBM)] * 10,
        out_specs=pl.BlockSpec(memory_space=pltpu.VMEM),
        scratch_shapes=[
            vmem((ROWS, D), BF16),
            vmem((D, COLS), BF16),
            vmem((AGENTS, COLS), F32),
            vmem((1, ROWS), jnp.int32),
            vmem((1, ROWS), jnp.int32),
            vmem((1, ROWS), F32),
            vmem((1, ROWS), F32),
            vmem((1, ROWS), jnp.int32),
            vmem((1, ROWS), F32),
            vmem((1, SAMPLES), jnp.int32),
            dma((10,)),
            vmem((COLS, ROWS), F32),
            vmem((COLS, ROWS), F32),
            vmem((COLS, ROWS), BF16),
            vmem((16, 8, D), F32),
            vmem((16, 8, D), BF16),
            vmem((16, 8, D), BF16),
            vmem((16, 8, D), BF16),
            vmem((8, 2, ROWS), F32),
            vmem((8, 3, ROWS), F32),
            vmem((8, 2, ROWS), F32),
            vmem((8, 2, 128), F32),
            vmem((8, 2, 128), F32),
            vmem((8, 1, 128), F32),
            vmem((8, 1, 128), F32),
            vmem((8, 1, 128), F32),
            vmem((8, 1, 128), F32),
            vmem((8, 1, 128), F32),
            vmem((8, 1, 128), F32),
            vmem((8, 1, 128), F32),
            vmem((2, NY, 8, LEFT), F32),
            vmem((2, NZ, 2, 8, D - LEFT), F32),
            vmem((NY, 8, LEFT), F32),
            vmem((NZ, 2, 8, D - LEFT), F32),
            vmem((NY, 8, LEFT), F32),
            vmem((NZ, 2, 8, D - LEFT), F32),
            vmem((NY, 8, LEFT), BF16),
            vmem((NZ, 2, 8, D - LEFT), BF16),
            vmem((NY, 8, LEFT), BF16),
            vmem((NZ, 2, 8, D - LEFT), BF16),
            vmem((2, NZ, 8, 384), F32),
            vmem((2, NY, 8, 256), F32),
            vmem((2, NZ, 8, 384), F32),
            vmem((2, NY, 8, 256), F32),
            dma((12,)),
            dma((12,)),
            dma((2, 6)),
            dma((2, 6)),
            dma((2, 12)),
            dma((3, 6)),
            dma((3, 4)),
            dma((3, 11)),
        ],
        compiler_params=pltpu.CompilerParams(
            collective_id=0, has_side_effects=True, vmem_limit_bytes=40 * 1024 * 1024
        ),
        name="step",
    )(
        *(
            pltpu.with_memory_space_constraint(x, pltpu.MemorySpace.HBM)
            for x in (
                hidden, head, bias, row(ids), row(actions), row(rewards), row(values), row(starts),
                row(ratio), row(samples),
            )
        )
    )
    return result.T


def solution(mesh):
    placed = (P("dp", None), P(None, "mp"), P(None, "mp")) + (P("dp"),) * 7
    return jax.shard_map(
        per_device, mesh=mesh, in_specs=placed, out_specs=P(None, "mp"), check_vma=False
    )
```

```python
import functools
import math

import jax
import jax.numpy as jnp
from jax import lax
from jax.experimental import pallas as pl
from jax.experimental.pallas import tpu as pltpu
from jax.sharding import PartitionSpec as P

D = 2560
A = 1024
AGENTS = 8
SEQ_LEN = 64
GAMMA = 0.99
TRACE_DECAY = 0.95
DAMPING = 0.001
RADIUS_SHARE = 0.001

MESH = pl.DeviceIdType.MESH
F32 = jnp.float32
BF16 = jnp.bfloat16
NY = 8
NZ = 4
NM = 8
ROWS = 512
SAMPLES = 2048
COLS = 128
LEFT = 1536
FAR_FIRST = (4, 3, 5, 2, 6, 1, 7)
NEAR_FIRST = (1, 7, 2, 6, 3, 5, 4)
ARRIVALS = (
    ("a", 1), ("a", 7), ("b", 1), ("a", 2), ("a", 6), ("b", 2), ("b", 3), ("a", 3), ("a", 5),
    ("a", 4),
)
CORE_ORDER = (
    ("a", 4), ("b", 3), ("a", 3), ("a", 5), ("b", 1), ("a", 2), ("a", 6), ("b", 2),
    ("a", 1), ("a", 7), ("a", 0), ("b", 0),
)


def kernel(
    hidden_in, head_in, bias_in, ids_in, actions_in, rewards_in, values_in, starts_in, ratio_in, samples_in,
    out,
    hidden, head, bias, ids, actions, rewards, values, starts, ratio, samples, loads,
    probs, weighted_spread, logit_grad, grad_t, resid_t, part, grad_hi, grad_lo, resid_hi,
    peak_box, centre_box, final_box, first_y, first_q, dots_m, dots_y, dots_q, adv_y, adv_q, curv_y, curv_q,
    core_a, core_b, send_a32, send_b32, y_a32, z_b32, send_a16, send_b16, y_a16, z_b16,
    own_a, own_b, z_a, y_b,
    small_s, small_r, rs_s, rs_r, rs_core, ag_s, ag_r, ag_line,
):
    dp, me_m = lax.axis_index("dp"), lax.axis_index("mp")
    core = lax.rem(dp, 2)
    y = lax.rem(dp // 2, NY)
    z = dp // (2 * NY)
    q = z * 2 + core

    def at_y(k):
        return ((z * NY + k) * 2 + core, me_m)

    def at_q(k):
        return ((k // 2 * NY + y) * 2 + lax.rem(k, 2), me_m)

    def at_z(k):
        return ((k * NY + y) * 2 + core, me_m)

    def at_m(k):
        return (dp, k)

    other = (dp + 1 - 2 * core, me_m)

    barrier = pltpu.get_barrier_semaphore()
    for o in range(1, 8):
        for target in (
            at_y(lax.rem(y + o, NY)),
            at_q(lax.rem(q + o, 8)),
            at_m(lax.rem(me_m + o, NM)),
        ):
            pl.semaphore_signal(barrier, inc=1, device_id=target, device_id_type=MESH)

    fetches = [
        pltpu.make_async_copy(src, dst, loads.at[k])
        for k, (src, dst) in enumerate(
            (
                (rewards_in, rewards), (values_in, values), (starts_in, starts),
                (hidden_in, hidden), (head_in, head), (bias_in, bias), (ids_in, ids),
                (actions_in, actions), (ratio_in, ratio), (samples_in, samples),
            )
        )
    ]
    for fetch in fetches:
        fetch.start()

    def copy(src, dst, send, recv, target):
        return pltpu.make_async_remote_copy(
            src_ref=src, dst_ref=dst, send_sem=send, recv_sem=recv,
            device_id=target, device_id_type=MESH,
        )

    def wait_sent(view, sem):
        copy(view, view, sem, sem, other).wait_send()

    def wait_come(view, sem):
        copy(view, view, sem, sem, other).wait_recv()

    def swap_start(n, box, me, place):
        for o in range(1, 8):
            copy(
                box.at[me], box.at[me], small_s.at[n], small_r.at[n], place(lax.rem(me + o, 8))
            ).start()

    def swap_wait(n, box, me, place):
        wait_come(box.at[0:7], small_r.at[n])
        wait_sent(box.at[0:7], small_s.at[n])

    def total(box):
        acc = box[0]
        for k in range(1, 8):
            acc = acc + box[k]
        return acc

    def lane_part(row):
        return row[:, 0:128] + row[:, 128:256] + row[:, 256:384] + row[:, 384:512]

    for fetch in fetches[:3]:
        fetch.wait()

    def ahead(x, s):
        return pltpu.roll(x, ROWS - s, 1)

    def wide(ref):
        return jnp.broadcast_to(ref[...].astype(F32), (8, ROWS))

    position = lax.broadcasted_iota(jnp.int32, (8, ROWS), 1)
    value = wide(values)
    ends = (lax.rem(position, SEQ_LEN) == SEQ_LEN - 1) | (ahead(wide(starts), 1) > 0.5)
    continues = jnp.where(ends, 0.0, 1.0)
    advantage = wide(rewards) + GAMMA * continues * ahead(value, 1) - value
    keeps = GAMMA * TRACE_DECAY * continues
    for s in (1, 2, 4, 8, 16, 32):
        advantage = advantage + keeps * ahead(advantage, s)
        keeps = keeps * ahead(keeps, s)
    advantage = advantage[0:1]
    adv_y[y] = lane_part(advantage)

    for fetch in fetches[3:]:
        fetch.wait()

    logits = jnp.dot(hidden[...], head[...], preferred_element_type=F32).T
    bias_t = bias[...].T
    agent = ids[...]
    for k in range(AGENTS):
        logits = logits + jnp.where(agent == k, bias_t[:, k : k + 1], 0.0)
    peak = jnp.max(logits, axis=0, keepdims=True)
    exponent = jnp.exp(logits - peak)
    peak_box[me_m, 0:1] = peak
    peak_box[me_m, 1:2] = jnp.sum(exponent, axis=0, keepdims=True)
    probs[...] = exponent
    pl.semaphore_wait(barrier, 21)
    swap_start(0, adv_y, y, at_y)
    swap_start(1, peak_box, me_m, at_m)

    local = samples[...] - dp * ROWS
    high = lax.shift_right_logical(local, 7)
    low = lax.bitwise_and(local, 127)
    high_hot = (lax.broadcasted_iota(jnp.int32, (8, SAMPLES), 0) == high).astype(F32).astype(BF16)
    low_hot = (lax.broadcasted_iota(jnp.int32, (128, SAMPLES), 0) == low).astype(F32).astype(BF16)
    tally = lax.dot_general(
        high_hot, low_hot, (((1,), (1,)), ((), ())), preferred_element_type=F32
    )
    count = jnp.concatenate([tally[0:1], tally[1:2], tally[2:3], tally[3:4]], axis=1)

    swap_wait(0, adv_y, y, at_y)
    adv_q[q] = total(adv_y)
    swap_start(2, adv_q, q, at_q)

    swap_wait(1, peak_box, me_m, at_m)
    row_peak = peak_box[0, 0:1]
    for k in range(1, NM):
        row_peak = jnp.maximum(row_peak, peak_box[k, 0:1])
    denominator = peak_box[0, 1:2] * jnp.exp(peak_box[0, 0:1] - row_peak)
    for k in range(1, NM):
        denominator = denominator + peak_box[k, 1:2] * jnp.exp(peak_box[k, 0:1] - row_peak)
    prob = probs[...] * (jnp.exp(peak - row_peak) / denominator)
    probs[...] = prob

    swap_wait(2, adv_q, q, at_q)
    tokens = ROWS * 64
    adv_mean = jnp.sum(total(adv_q), axis=1, keepdims=True) / tokens
    weight = ratio[...] * (advantage - adv_mean) / tokens
    picked = lax.broadcasted_iota(jnp.int32, (COLS, ROWS), 0) == actions[...] - me_m * COLS
    logit_grad[...] = (weight * (jnp.where(picked, 1.0, 0.0) - prob)).astype(BF16)

    def project(tiles):
        for j in tiles:
            cols = slice(512 * j, 512 * (j + 1))
            part[:, :, cols] = jnp.dot(
                logit_grad[...], hidden[:, cols], preferred_element_type=F32
            ).reshape(16, 8, 512)

    def scatter(n, send_a, send_b, y_a, z_b, between):
        def core_copy(kind, o):
            if kind == "a":
                k = (1 - core) * 8 + lax.rem(y + o, NY)
                return copy(
                    part.at[k, :, 0:LEFT], core_a.at[n, o], rs_s.at[n, 0], rs_core.at[n, o], other
                )
            k = (1 - core) * 8 + lax.rem(z + o, NZ) * 2
            return copy(
                part.at[pl.ds(k, 2), :, LEFT:D], core_b.at[n, o],
                rs_s.at[n, 1], rs_core.at[n, 8 + o], other,
            )

        for tiles, part_kind in ((range(3), "a"), (range(3, 5), "b")):
            project(tiles)
            for kind, o in CORE_ORDER:
                if kind == part_kind:
                    core_copy(kind, o).start()
        for kind, o in CORE_ORDER:
            core_copy(kind, o).wait_recv()
            if kind == "a":
                k = lax.rem(y + o, NY)
                term = part[core * 8 + k, :, 0:LEFT] + core_a[n, o]
                if o == 0:
                    acc_a = term
                    continue
                send_a[o] = term.astype(send_a.dtype)
                copy(send_a.at[o], y_a.at[o], rs_s.at[n, 2], rs_r.at[n, 2], at_y(k)).start()
            else:
                k = lax.rem(z + o, NZ)
                term = part[pl.ds(core * 8 + 2 * k, 2), :, LEFT:D] + core_b[n, o]
                if o == 0:
                    acc_b = term
                    continue
                send_b[o] = term.astype(send_b.dtype)
                copy(send_b.at[o], z_b.at[o], rs_s.at[n, 3], rs_r.at[n, 3], at_z(k)).start()
        wait_come(z_b.at[1:4], rs_r.at[n, 3])
        for o in (1, 2, 3):
            acc_b = acc_b + z_b[o].astype(F32)
        for k in range(NY):
            own_b[n, k] = acc_b[k // 4, :, 256 * (k % 4) : 256 * (k % 4 + 1)]
        for o in FAR_FIRST:
            k = lax.rem(y + o, NY)
            copy(own_b.at[n, k], y_b.at[n, o], rs_s.at[n, 4], rs_r.at[n, 4], at_y(k)).start()
        between()
        wait_come(y_a.at[1:8], rs_r.at[n, 2])
        for o in NEAR_FIRST:
            acc_a = acc_a + y_a[o].astype(F32)
        for k in range(NZ):
            own_a[n, k] = acc_a[:, 384 * k : 384 * (k + 1)]
        for o in (3, 2, 1):
            k = lax.rem(z + o, NZ)
            copy(own_a.at[n, k], z_a.at[n, o], rs_s.at[n, 5], rs_r.at[n, 5], at_z(k)).start()
        shard_b = own_b[n, y]
        wait_come(y_b.at[n, 1:8], rs_r.at[n, 4])
        for o in NEAR_FIRST:
            shard_b = shard_b + y_b[n, o]
        shard_a = own_a[n, z]
        wait_come(z_a.at[n, 1:4], rs_r.at[n, 5])
        for o in (1, 2, 3):
            shard_a = shard_a + z_a[n, o]
        return shard_a, shard_b

    def scatter_end(n, send_a, send_b):
        wait_sent(part.at[0:8, :, 0:LEFT], rs_s.at[n, 0])
        wait_sent(part.at[0:8, :, LEFT:D], rs_s.at[n, 1])
        wait_sent(send_a.at[1:8], rs_s.at[n, 2])
        wait_sent(send_b.at[1:4], rs_s.at[n, 3])
        wait_sent(own_b.at[n, 1:8], rs_s.at[n, 4])
        wait_sent(own_a.at[n, 1:4], rs_s.at[n, 5])

    def spot_a(full, ky, kz):
        return full.at[core * 8 + ky, :, pl.ds(pl.multiple_of(kz * 384, 128), 384)]

    def spot_b(full, ky, kz):
        columns = pl.ds(pl.multiple_of(LEFT + lax.rem(ky, 4) * 256, 128), 256)
        return full.at[core * 8 + 2 * kz + ky // 4, :, columns]

    def line_a(full, kc, ky):
        return full.at[kc * 8 + ky, :, 0:LEFT]

    def line_b(full, kc, kz):
        return full.at[pl.ds(kc * 8 + 2 * kz, 2), :, LEFT:D]

    def gather_start(n, full):
        def begin(ref, kind, recv, target):
            copy(ref, ref, ag_s.at[n, kind], recv, target).start()

        mine = core * 8 + y
        for o in (3, 2, 1):
            begin(spot_a(full, y, z), 0, ag_r.at[n, 0], at_z(lax.rem(z + o, NZ)))
        for o in FAR_FIRST:
            begin(spot_b(full, y, z), 1, ag_r.at[n, 1], at_y(lax.rem(y + o, NY)))
        wait_come(full.at[mine, :, 0 : 3 * 384], ag_r.at[n, 0])
        for o in FAR_FIRST:
            begin(line_a(full, core, y), 2, ag_line.at[n, o], at_y(lax.rem(y + o, NY)))
        begin(line_a(full, core, y), 4, ag_r.at[n, 2], other)
        wait_come(full.at[mine, :, 0 : 7 * 256], ag_r.at[n, 1])
        for o in (3, 2, 1):
            begin(line_b(full, core, z), 3, ag_line.at[n, 7 + o], at_z(lax.rem(z + o, NZ)))
        begin(line_b(full, core, z), 5, ag_r.at[n, 3], other)

    def gather_wait(n, full):
        def arrive(ref, line, kind, recv):
            wait_come(ref, ag_line.at[n, line])
            copy(ref, ref, ag_s.at[n, kind], recv, other).start()

        for kind, o in ARRIVALS:
            if kind == "a":
                arrive(line_a(full, core, lax.rem(y + NY - o, NY)), o, 4, ag_r.at[n, 2])
            else:
                arrive(line_b(full, core, lax.rem(z + NZ - o, NZ)), 7 + o, 5, ag_r.at[n, 3])
        wait_come(full.at[pl.ds((1 - core) * 8, 8), :, 0:LEFT], ag_r.at[n, 2])
        wait_come(full.at[pl.ds((1 - core) * 8, 8), :, LEFT:D], ag_r.at[n, 3])

    def gather_end(n, full):
        wait_sent(full.at[0, :, 0 : 3 * 384], ag_s.at[n, 0])
        wait_sent(full.at[0, :, 0 : 7 * 256], ag_s.at[n, 1])
        wait_sent(full.at[0:7, :, 0:LEFT], ag_s.at[n, 2])
        wait_sent(full.at[0:6, :, LEFT:D], ag_s.at[n, 3])
        wait_sent(full.at[0:8, :, 0:LEFT], ag_s.at[n, 4])
        wait_sent(full.at[0:8, :, LEFT:D], ag_s.at[n, 5])

    def keep(full, shards):
        shard_a, shard_b = shards
        full[core * 8 + y, :, pl.ds(pl.multiple_of(z * 384, 128), 384)] = shard_a.astype(BF16)
        columns = pl.ds(pl.multiple_of(LEFT + lax.rem(y, 4) * 256, 128), 256)
        full[core * 8 + 2 * z + y // 4, :, columns] = shard_b.astype(BF16)

    def lift(vector):
        return lax.dot_general(
            vector.reshape(COLS, D).astype(BF16), hidden[...], (((1,), (1,)), ((), ())),
            preferred_element_type=F32,
        )

    def folded(left, right):
        terms = [
            l[:, k : k + 128] * r[:, k : k + 128]
            for l, r in zip(left, right)
            for k in range(0, l.shape[1], 128)
        ]
        return jnp.sum(sum(terms[1:], terms[0]), axis=0, keepdims=True)

    grad_piece = scatter(0, send_a32, send_b32, y_a32, z_b32, lambda: None)
    keep(grad_hi, grad_piece)
    keep(grad_lo, [x - x.astype(BF16).astype(F32) for x in grad_piece])
    gather_start(0, grad_hi)
    gather_wait(0, grad_hi)
    scatter_end(0, send_a32, send_b32)

    def local_moments(box, prob, lifted):
        mass = jnp.sum(prob, axis=0, keepdims=True)
        moment = jnp.sum(prob * lifted, axis=0, keepdims=True)
        spread = lifted - share(moment, mass)
        box[me_m, 0:1] = moment
        box[me_m, 1:2] = jnp.sum(prob * spread * spread, axis=0, keepdims=True)
        return spread

    def share(moment, mass):
        return jnp.where(mass > 0.0, moment / jnp.where(mass > 0.0, mass, 1.0), 0.0)

    def row_aways(box):
        masses = [
            peak_box[k, 1:2] * (jnp.exp(peak_box[k, 0:1] - row_peak) / denominator)
            for k in range(NM)
        ]
        centre = total(box)[0:1]
        return masses, [share(box[k, 0:1], m) - centre for k, m in enumerate(masses)]

    def row_sum(box, row, masses, left, right):
        acc = total(box)[row : row + 1]
        for m, l, r in zip(masses, left, right):
            acc = acc + m * l * r
        return acc

    lifted = lift(grad_hi[...].astype(F32))
    prob = probs[...]
    weighted_spread[...] = prob * local_moments(centre_box, prob, lifted)
    centre_box[me_m, 2:3] = jnp.concatenate(
        [folded(grad_piece, grad_piece), jnp.zeros((1, ROWS - 128), F32)], axis=1
    )
    swap_start(3, centre_box, me_m, at_m)
    swap_wait(3, centre_box, me_m, at_m)
    centre = total(centre_box)[0:1]
    logit_grad[...] = (count * (prob * (lifted - centre))).astype(BF16)
    masses, aways = row_aways(centre_box)
    first_y[y, 0:1] = lane_part(count * row_sum(centre_box, 1, masses, aways, aways))
    first_y[y, 1:2] = total(centre_box)[2:3, 0:128]
    swap_start(4, first_y, y, at_y)

    def pass_on():
        swap_wait(4, first_y, y, at_y)
        first_q[q] = total(first_y)
        swap_start(5, first_q, q, at_q)

    summed = scatter(1, send_a16, send_b16, y_a16, z_b16, pass_on)
    swap_wait(5, first_q, q, at_q)
    dots = jnp.sum(total(first_q), axis=1, keepdims=True)
    rr = dots[1:2]
    curvature = dots[0:1] / (SAMPLES * 64) + DAMPING * rr
    step = rr / curvature
    quad = step * step * curvature
    resid_piece = [
        g - step * (f / (SAMPLES * 64) + DAMPING * g) for f, g in zip(summed, grad_piece)
    ]
    keep(resid_hi, resid_piece)
    dots_m[me_m] = folded(resid_piece, resid_piece)
    swap_start(6, dots_m, me_m, at_m)
    gather_start(1, resid_hi)
    swap_wait(6, dots_m, me_m, at_m)
    dots_y[y] = total(dots_m)
    swap_start(7, dots_y, y, at_y)
    swap_wait(7, dots_y, y, at_y)
    gather_wait(1, resid_hi)

    lifted = lift(resid_hi[...].astype(F32))
    spread = local_moments(final_box, probs[...], lifted)
    final_box[me_m, 2:3] = jnp.sum(weighted_spread[...] * spread, axis=0, keepdims=True)
    swap_start(9, final_box, me_m, at_m)
    dots_q[q] = total(dots_y)
    swap_start(8, dots_q, q, at_q)
    gather_start(2, grad_lo)
    swap_wait(9, final_box, me_m, at_m)
    _, resid_aways = row_aways(final_box)
    curv_y[y, 0:1] = lane_part(count * row_sum(final_box, 1, masses, resid_aways, resid_aways))
    curv_y[y, 1:2] = lane_part(count * row_sum(final_box, 2, masses, resid_aways, aways))
    swap_start(10, curv_y, y, at_y)
    swap_wait(8, dots_q, q, at_q)
    rr_next = jnp.sum(total(dots_q), axis=1, keepdims=True)
    beta = rr_next / rr
    swap_wait(10, curv_y, y, at_y)
    curv_q[q] = total(curv_y)
    swap_start(11, curv_q, q, at_q)
    gather_wait(2, grad_lo)
    scatter_end(1, send_a16, send_b16)
    for n, full in enumerate((grad_hi, resid_hi, grad_lo)):
        gather_end(n, full)
    for k in range(16):
        part[k] = grad_hi[k].astype(F32) + grad_lo[k].astype(F32)
    for j in range(D // 128):
        cols = slice(128 * j, 128 * (j + 1))
        grad_t[cols] = part[:, :, cols].reshape(COLS, 128).T
        resid_t[cols] = resid_hi[:, :, cols].astype(F32).reshape(COLS, 128).T
    swap_wait(11, curv_q, q, at_q)
    curves = jnp.sum(total(curv_q), axis=1, keepdims=True)
    curvature = curves[0:1] + 2.0 * beta * curves[1:2] + beta * beta * dots[0:1]
    curvature = curvature / (SAMPLES * 64)
    curvature = curvature + DAMPING * (rr_next + beta * beta * rr)
    last = rr_next / curvature
    quad = quad + last * last * curvature
    scale = jnp.sqrt(D * A * RADIUS_SHARE / quad)
    of_grad = (step + last * beta) * scale
    of_resid = last * scale
    out[...] = of_grad * grad_t[...] + of_resid * resid_t[...]


def per_device(hidden, head, bias, ids, actions, rewards, values, starts, ratio, samples):
    dma = pltpu.SemaphoreType.DMA
    vmem = pltpu.VMEM

    def row(x):
        return x.reshape(1, -1)

    return pl.pallas_call(
        kernel,
        out_shape=jax.ShapeDtypeStruct((D, COLS), F32),
        in_specs=[pl.BlockSpec(memory_space=pltpu.MemorySpace.HBM)] * 10,
        out_specs=pl.BlockSpec(memory_space=pltpu.VMEM),
        scratch_shapes=[
            vmem((ROWS, D), BF16),
            vmem((D, COLS), BF16),
            vmem((AGENTS, COLS), F32),
            vmem((1, ROWS), jnp.int32),
            vmem((1, ROWS), jnp.int32),
            vmem((1, ROWS), F32),
            vmem((1, ROWS), F32),
            vmem((1, ROWS), jnp.int32),
            vmem((1, ROWS), F32),
            vmem((1, SAMPLES), jnp.int32),
            dma((10,)),
            vmem((COLS, ROWS), F32),
            vmem((COLS, ROWS), F32),
            vmem((COLS, ROWS), BF16),
            vmem((D, COLS), F32),
            vmem((D, COLS), F32),
            vmem((16, 8, D), F32),
            vmem((16, 8, D), BF16),
            vmem((16, 8, D), BF16),
            vmem((16, 8, D), BF16),
            vmem((8, 2, ROWS), F32),
            vmem((8, 3, ROWS), F32),
            vmem((8, 3, ROWS), F32),
            vmem((8, 2, 128), F32),
            vmem((8, 2, 128), F32),
            vmem((8, 1, 128), F32),
            vmem((8, 1, 128), F32),
            vmem((8, 1, 128), F32),
            vmem((8, 1, 128), F32),
            vmem((8, 1, 128), F32),
            vmem((8, 2, 128), F32),
            vmem((8, 2, 128), F32),
            vmem((2, NY, 8, LEFT), F32),
            vmem((2, NZ, 2, 8, D - LEFT), F32),
            vmem((NY, 8, LEFT), F32),
            vmem((NZ, 2, 8, D - LEFT), F32),
            vmem((NY, 8, LEFT), F32),
            vmem((NZ, 2, 8, D - LEFT), F32),
            vmem((NY, 8, LEFT), BF16),
            vmem((NZ, 2, 8, D - LEFT), BF16),
            vmem((NY, 8, LEFT), BF16),
            vmem((NZ, 2, 8, D - LEFT), BF16),
            vmem((2, NZ, 8, 384), F32),
            vmem((2, NY, 8, 256), F32),
            vmem((2, NZ, 8, 384), F32),
            vmem((2, NY, 8, 256), F32),
            dma((12,)),
            dma((12,)),
            dma((2, 6)),
            dma((2, 6)),
            dma((2, 12)),
            dma((3, 6)),
            dma((3, 4)),
            dma((3, 11)),
        ],
        compiler_params=pltpu.CompilerParams(
            collective_id=0, has_side_effects=True, vmem_limit_bytes=40 * 1024 * 1024
        ),
        name="step",
    )(
        *(
            pltpu.with_memory_space_constraint(x, pltpu.MemorySpace.HBM)
            for x in (
                hidden, head, bias, row(ids), row(actions), row(rewards), row(values), row(starts),
                row(ratio), row(samples),
            )
        )
    )


def solution(mesh):
    placed = (P("dp", None), P(None, "mp"), P(None, "mp")) + (P("dp"),) * 7
    return jax.shard_map(
        per_device, mesh=mesh, in_specs=placed, out_specs=P(None, "mp"), check_vma=False
    )
```

```python
import functools
import math

import jax
import jax.numpy as jnp
from jax import lax
from jax.experimental import pallas as pl
from jax.experimental.pallas import tpu as pltpu
from jax.sharding import PartitionSpec as P

D = 2560
A = 1024
AGENTS = 8
SEQ_LEN = 64
GAMMA = 0.99
TRACE_DECAY = 0.95
DAMPING = 0.001
RADIUS_SHARE = 0.001

MESH = pl.DeviceIdType.MESH
F32 = jnp.float32
BF16 = jnp.bfloat16
NY = 8
NZ = 4
NM = 8
ROWS = 512
SAMPLES = 2048
COLS = 128
LEFT = 1536
FAR_FIRST = (4, 3, 5, 2, 6, 1, 7)
NEAR_FIRST = (1, 7, 2, 6, 3, 5, 4)
ARRIVALS = (
    ("a", 1), ("a", 7), ("b", 1), ("a", 2), ("a", 6), ("b", 2), ("b", 3), ("a", 3), ("a", 5),
    ("a", 4),
)
CORE_ORDER = (
    ("a", 4), ("b", 3), ("a", 3), ("a", 5), ("b", 1), ("a", 2), ("a", 6), ("b", 2),
    ("a", 1), ("a", 7), ("a", 0), ("b", 0),
)


def kernel(
    hidden_in, head_in, bias_in, ids_in, actions_in, rewards_in, values_in, starts_in, ratio_in, samples_in,
    out,
    hidden, head, bias, ids, actions, rewards, values, starts, ratio, samples, loads,
    probs, weighted_spread, logit_grad, grad_t, resid_t, part, grad_hi, grad_lo, resid_hi,
    peak_box, centre_box, final_box, first_y, first_q, dots_m, dots_y, dots_q, adv_y, adv_q, curv_y, curv_q,
    core_a, core_b, send_a0, send_b0, y_a0, z_b0, send_a1, send_b1, y_a1, z_b1,
    own_a, own_b, z_a, y_b,
    rest_a, rest_b, rest_y, rest_z, rest_own_a, rest_own_b, rest_za, rest_yb, rest_s, rest_r,
    small_s, small_r, rs_s, rs_r, rs_core, ag_s, ag_r, ag_line,
):
    dp, me_m = lax.axis_index("dp"), lax.axis_index("mp")
    core = lax.rem(dp, 2)
    y = lax.rem(dp // 2, NY)
    z = dp // (2 * NY)
    q = z * 2 + core

    def at_y(k):
        return ((z * NY + k) * 2 + core, me_m)

    def at_q(k):
        return ((k // 2 * NY + y) * 2 + lax.rem(k, 2), me_m)

    def at_z(k):
        return ((k * NY + y) * 2 + core, me_m)

    def at_m(k):
        return (dp, k)

    other = (dp + 1 - 2 * core, me_m)

    barrier = pltpu.get_barrier_semaphore()
    for o in range(1, 8):
        for target in (
            at_y(lax.rem(y + o, NY)),
            at_q(lax.rem(q + o, 8)),
            at_m(lax.rem(me_m + o, NM)),
        ):
            pl.semaphore_signal(barrier, inc=1, device_id=target, device_id_type=MESH)

    fetches = [
        pltpu.make_async_copy(src, dst, loads.at[k])
        for k, (src, dst) in enumerate(
            (
                (rewards_in, rewards), (values_in, values), (starts_in, starts),
                (hidden_in, hidden), (head_in, head), (bias_in, bias), (ids_in, ids),
                (actions_in, actions), (ratio_in, ratio), (samples_in, samples),
            )
        )
    ]
    for fetch in fetches:
        fetch.start()

    def copy(src, dst, send, recv, target):
        return pltpu.make_async_remote_copy(
            src_ref=src, dst_ref=dst, send_sem=send, recv_sem=recv,
            device_id=target, device_id_type=MESH,
        )

    def wait_sent(view, sem):
        copy(view, view, sem, sem, other).wait_send()

    def wait_come(view, sem):
        copy(view, view, sem, sem, other).wait_recv()

    def swap_start(n, box, me, place):
        for o in range(1, 8):
            copy(
                box.at[me], box.at[me], small_s.at[n], small_r.at[n], place(lax.rem(me + o, 8))
            ).start()

    def swap_wait(n, box, me, place):
        wait_come(box.at[0:7], small_r.at[n])
        wait_sent(box.at[0:7], small_s.at[n])

    def total(box):
        acc = box[0]
        for k in range(1, 8):
            acc = acc + box[k]
        return acc

    def lane_part(row):
        return row[:, 0:128] + row[:, 128:256] + row[:, 256:384] + row[:, 384:512]

    for fetch in fetches[:3]:
        fetch.wait()

    def ahead(x, s):
        return pltpu.roll(x, ROWS - s, 1)

    def wide(ref):
        return jnp.broadcast_to(ref[...].astype(F32), (8, ROWS))

    position = lax.broadcasted_iota(jnp.int32, (8, ROWS), 1)
    value = wide(values)
    ends = (lax.rem(position, SEQ_LEN) == SEQ_LEN - 1) | (ahead(wide(starts), 1) > 0.5)
    continues = jnp.where(ends, 0.0, 1.0)
    advantage = wide(rewards) + GAMMA * continues * ahead(value, 1) - value
    keeps = GAMMA * TRACE_DECAY * continues
    for s in (1, 2, 4, 8, 16, 32):
        advantage = advantage + keeps * ahead(advantage, s)
        keeps = keeps * ahead(keeps, s)
    advantage = advantage[0:1]
    adv_y[y] = lane_part(advantage)

    for fetch in fetches[3:]:
        fetch.wait()

    logits = jnp.dot(hidden[...], head[...], preferred_element_type=F32).T
    bias_t = bias[...].T
    agent = ids[...]
    for k in range(AGENTS):
        logits = logits + jnp.where(agent == k, bias_t[:, k : k + 1], 0.0)
    peak = jnp.max(logits, axis=0, keepdims=True)
    exponent = jnp.exp(logits - peak)
    peak_box[me_m, 0:1] = peak
    peak_box[me_m, 1:2] = jnp.sum(exponent, axis=0, keepdims=True)
    probs[...] = exponent
    pl.semaphore_wait(barrier, 21)
    swap_start(0, adv_y, y, at_y)
    swap_start(1, peak_box, me_m, at_m)

    local = samples[...] - dp * ROWS
    high = lax.shift_right_logical(local, 7)
    low = lax.bitwise_and(local, 127)
    high_hot = (lax.broadcasted_iota(jnp.int32, (8, SAMPLES), 0) == high).astype(F32).astype(BF16)
    low_hot = (lax.broadcasted_iota(jnp.int32, (128, SAMPLES), 0) == low).astype(F32).astype(BF16)
    tally = lax.dot_general(
        high_hot, low_hot, (((1,), (1,)), ((), ())), preferred_element_type=F32
    )
    count = jnp.concatenate([tally[0:1], tally[1:2], tally[2:3], tally[3:4]], axis=1)

    swap_wait(0, adv_y, y, at_y)
    adv_q[q] = total(adv_y)
    swap_start(2, adv_q, q, at_q)

    swap_wait(1, peak_box, me_m, at_m)
    row_peak = peak_box[0, 0:1]
    for k in range(1, NM):
        row_peak = jnp.maximum(row_peak, peak_box[k, 0:1])
    denominator = peak_box[0, 1:2] * jnp.exp(peak_box[0, 0:1] - row_peak)
    for k in range(1, NM):
        denominator = denominator + peak_box[k, 1:2] * jnp.exp(peak_box[k, 0:1] - row_peak)
    prob = probs[...] * (jnp.exp(peak - row_peak) / denominator)
    probs[...] = prob

    swap_wait(2, adv_q, q, at_q)
    tokens = ROWS * 64
    adv_mean = jnp.sum(total(adv_q), axis=1, keepdims=True) / tokens
    weight = ratio[...] * (advantage - adv_mean) / tokens
    picked = lax.broadcasted_iota(jnp.int32, (COLS, ROWS), 0) == actions[...] - me_m * COLS
    logit_grad[...] = (weight * (jnp.where(picked, 1.0, 0.0) - prob)).astype(BF16)

    def project(tiles):
        for j in tiles:
            cols = slice(512 * j, 512 * (j + 1))
            part[:, :, cols] = jnp.dot(
                logit_grad[...], hidden[:, cols], preferred_element_type=F32
            ).reshape(16, 8, 512)

    def scatter(n, send_a, send_b, y_a, z_b, between, then):
        def core_copy(kind, o):
            if kind == "a":
                k = (1 - core) * 8 + lax.rem(y + o, NY)
                return copy(
                    part.at[k, :, 0:LEFT], core_a.at[n, o], rs_s.at[n, 0], rs_core.at[n, o], other
                )
            k = (1 - core) * 8 + lax.rem(z + o, NZ) * 2
            return copy(
                part.at[pl.ds(k, 2), :, LEFT:D], core_b.at[n, o],
                rs_s.at[n, 1], rs_core.at[n, 8 + o], other,
            )

        for tiles, part_kind in ((range(3), "a"), (range(3, 5), "b")):
            project(tiles)
            for kind, o in CORE_ORDER:
                if kind == part_kind:
                    core_copy(kind, o).start()
        for kind, o in CORE_ORDER:
            core_copy(kind, o).wait_recv()
            if kind == "a":
                k = lax.rem(y + o, NY)
                term = part[core * 8 + k, :, 0:LEFT] + core_a[n, o]
                if o == 0:
                    acc_a = term
                    continue
                send_a[o] = term.astype(BF16)
                if n == 0:
                    rest_a[o] = (term - term.astype(BF16).astype(F32)).astype(BF16)
                copy(send_a.at[o], y_a.at[o], rs_s.at[n, 2], rs_r.at[n, 2], at_y(k)).start()
            else:
                k = lax.rem(z + o, NZ)
                term = part[pl.ds(core * 8 + 2 * k, 2), :, LEFT:D] + core_b[n, o]
                if o == 0:
                    acc_b = term
                    continue
                send_b[o] = term.astype(BF16)
                if n == 0:
                    rest_b[o] = (term - term.astype(BF16).astype(F32)).astype(BF16)
                copy(send_b.at[o], z_b.at[o], rs_s.at[n, 3], rs_r.at[n, 3], at_z(k)).start()
        wait_come(z_b.at[1:4], rs_r.at[n, 3])
        for o in (1, 2, 3):
            acc_b = acc_b + z_b[o].astype(F32)
        for k in range(NY):
            own_b[n, k] = acc_b[k // 4, :, 256 * (k % 4) : 256 * (k % 4 + 1)]
        for o in FAR_FIRST:
            k = lax.rem(y + o, NY)
            copy(own_b.at[n, k], y_b.at[n, o], rs_s.at[n, 4], rs_r.at[n, 4], at_y(k)).start()
        between()
        wait_come(y_a.at[1:8], rs_r.at[n, 2])
        for o in NEAR_FIRST:
            acc_a = acc_a + y_a[o].astype(F32)
        for k in range(NZ):
            own_a[n, k] = acc_a[:, 384 * k : 384 * (k + 1)]
        for o in (3, 2, 1):
            k = lax.rem(z + o, NZ)
            copy(own_a.at[n, k], z_a.at[n, o], rs_s.at[n, 5], rs_r.at[n, 5], at_z(k)).start()
        then()
        shard_b = own_b[n, y]
        wait_come(y_b.at[n, 1:8], rs_r.at[n, 4])
        for o in NEAR_FIRST:
            shard_b = shard_b + y_b[n, o]
        shard_a = own_a[n, z]
        wait_come(z_a.at[n, 1:4], rs_r.at[n, 5])
        for o in (1, 2, 3):
            shard_a = shard_a + z_a[n, o]
        return shard_a, shard_b

    def rest_start():
        for o in FAR_FIRST:
            copy(
                rest_a.at[o], rest_y.at[o], rest_s.at[0], rest_r.at[0], at_y(lax.rem(y + o, NY))
            ).start()
        for o in (3, 2, 1):
            copy(
                rest_b.at[o], rest_z.at[o], rest_s.at[1], rest_r.at[1], at_z(lax.rem(z + o, NZ))
            ).start()

    def rest_turn():
        wait_come(rest_z.at[1:4], rest_r.at[1])
        acc = rest_z[1].astype(F32) + rest_z[2].astype(F32) + rest_z[3].astype(F32)
        for k in range(NY):
            cols = slice(256 * (k % 4), 256 * (k % 4 + 1))
            rest_own_b[k] = acc[k // 4, :, cols].astype(BF16)
        for o in FAR_FIRST:
            k = lax.rem(y + o, NY)
            copy(rest_own_b.at[k], rest_yb.at[o], rest_s.at[2], rest_r.at[2], at_y(k)).start()
        wait_come(rest_y.at[1:8], rest_r.at[0])
        acc = rest_y[1].astype(F32)
        for o in range(2, 8):
            acc = acc + rest_y[o].astype(F32)
        for k in range(NZ):
            rest_own_a[k] = acc[:, 384 * k : 384 * (k + 1)].astype(BF16)
        for o in (3, 2, 1):
            k = lax.rem(z + o, NZ)
            copy(rest_own_a.at[k], rest_za.at[o], rest_s.at[3], rest_r.at[3], at_z(k)).start()

    def rest_wait():
        rest_of_b = rest_own_b[y].astype(F32)
        wait_come(rest_yb.at[1:8], rest_r.at[2])
        for o in range(1, 8):
            rest_of_b = rest_of_b + rest_yb[o].astype(F32)
        rest_of_a = rest_own_a[z].astype(F32)
        wait_come(rest_za.at[1:4], rest_r.at[3])
        for o in range(1, 4):
            rest_of_a = rest_of_a + rest_za[o].astype(F32)
        wait_sent(rest_a.at[1:8], rest_s.at[0])
        wait_sent(rest_b.at[1:4], rest_s.at[1])
        wait_sent(rest_own_b.at[1:8], rest_s.at[2])
        wait_sent(rest_own_a.at[1:4], rest_s.at[3])
        return rest_of_a, rest_of_b

    def scatter_end(n, send_a, send_b):
        wait_sent(part.at[0:8, :, 0:LEFT], rs_s.at[n, 0])
        wait_sent(part.at[0:8, :, LEFT:D], rs_s.at[n, 1])
        wait_sent(send_a.at[1:8], rs_s.at[n, 2])
        wait_sent(send_b.at[1:4], rs_s.at[n, 3])
        wait_sent(own_b.at[n, 1:8], rs_s.at[n, 4])
        wait_sent(own_a.at[n, 1:4], rs_s.at[n, 5])

    def spot_a(full, ky, kz):
        return full.at[core * 8 + ky, :, pl.ds(pl.multiple_of(kz * 384, 128), 384)]

    def spot_b(full, ky, kz):
        columns = pl.ds(pl.multiple_of(LEFT + lax.rem(ky, 4) * 256, 128), 256)
        return full.at[core * 8 + 2 * kz + ky // 4, :, columns]

    def line_a(full, kc, ky):
        return full.at[kc * 8 + ky, :, 0:LEFT]

    def line_b(full, kc, kz):
        return full.at[pl.ds(kc * 8 + 2 * kz, 2), :, LEFT:D]

    def gather_start(n, full):
        def begin(ref, kind, recv, target):
            copy(ref, ref, ag_s.at[n, kind], recv, target).start()

        mine = core * 8 + y
        for o in (3, 2, 1):
            begin(spot_a(full, y, z), 0, ag_r.at[n, 0], at_z(lax.rem(z + o, NZ)))
        for o in FAR_FIRST:
            begin(spot_b(full, y, z), 1, ag_r.at[n, 1], at_y(lax.rem(y + o, NY)))
        wait_come(full.at[mine, :, 0 : 3 * 384], ag_r.at[n, 0])
        for o in FAR_FIRST:
            begin(line_a(full, core, y), 2, ag_line.at[n, o], at_y(lax.rem(y + o, NY)))
        begin(line_a(full, core, y), 4, ag_r.at[n, 2], other)
        wait_come(full.at[mine, :, 0 : 7 * 256], ag_r.at[n, 1])
        for o in (3, 2, 1):
            begin(line_b(full, core, z), 3, ag_line.at[n, 7 + o], at_z(lax.rem(z + o, NZ)))
        begin(line_b(full, core, z), 5, ag_r.at[n, 3], other)

    def gather_wait(n, full):
        def arrive(ref, line, kind, recv):
            wait_come(ref, ag_line.at[n, line])
            copy(ref, ref, ag_s.at[n, kind], recv, other).start()

        for kind, o in ARRIVALS:
            if kind == "a":
                arrive(line_a(full, core, lax.rem(y + NY - o, NY)), o, 4, ag_r.at[n, 2])
            else:
                arrive(line_b(full, core, lax.rem(z + NZ - o, NZ)), 7 + o, 5, ag_r.at[n, 3])
        wait_come(full.at[pl.ds((1 - core) * 8, 8), :, 0:LEFT], ag_r.at[n, 2])
        wait_come(full.at[pl.ds((1 - core) * 8, 8), :, LEFT:D], ag_r.at[n, 3])

    def gather_end(n, full):
        wait_sent(full.at[0, :, 0 : 3 * 384], ag_s.at[n, 0])
        wait_sent(full.at[0, :, 0 : 7 * 256], ag_s.at[n, 1])
        wait_sent(full.at[0:7, :, 0:LEFT], ag_s.at[n, 2])
        wait_sent(full.at[0:6, :, LEFT:D], ag_s.at[n, 3])
        wait_sent(full.at[0:8, :, 0:LEFT], ag_s.at[n, 4])
        wait_sent(full.at[0:8, :, LEFT:D], ag_s.at[n, 5])

    def keep(full, shards):
        shard_a, shard_b = shards
        full[core * 8 + y, :, pl.ds(pl.multiple_of(z * 384, 128), 384)] = shard_a.astype(BF16)
        columns = pl.ds(pl.multiple_of(LEFT + lax.rem(y, 4) * 256, 128), 256)
        full[core * 8 + 2 * z + y // 4, :, columns] = shard_b.astype(BF16)

    def lift(vector):
        return lax.dot_general(
            vector.reshape(COLS, D).astype(BF16), hidden[...], (((1,), (1,)), ((), ())),
            preferred_element_type=F32,
        )

    def folded(left, right):
        terms = [
            l[:, k : k + 128] * r[:, k : k + 128]
            for l, r in zip(left, right)
            for k in range(0, l.shape[1], 128)
        ]
        return jnp.sum(sum(terms[1:], terms[0]), axis=0, keepdims=True)

    grad_first = scatter(0, send_a0, send_b0, y_a0, z_b0, lambda: None, rest_start)
    keep(grad_hi, grad_first)
    gather_start(0, grad_hi)
    rest_turn()
    gather_wait(0, grad_hi)
    scatter_end(0, send_a0, send_b0)
    grad_piece = [x + r for x, r in zip(grad_first, rest_wait())]
    keep(grad_lo, [x - f.astype(BF16).astype(F32) for x, f in zip(grad_piece, grad_first)])

    def local_moments(box, prob, lifted):
        mass = jnp.sum(prob, axis=0, keepdims=True)
        moment = jnp.sum(prob * lifted, axis=0, keepdims=True)
        spread = lifted - share(moment, mass)
        box[me_m, 0:1] = moment
        box[me_m, 1:2] = jnp.sum(prob * spread * spread, axis=0, keepdims=True)
        return spread

    def share(moment, mass):
        return jnp.where(mass > 0.0, moment / jnp.where(mass > 0.0, mass, 1.0), 0.0)

    def row_aways(box):
        masses = [
            peak_box[k, 1:2] * (jnp.exp(peak_box[k, 0:1] - row_peak) / denominator)
            for k in range(NM)
        ]
        centre = total(box)[0:1]
        return masses, [share(box[k, 0:1], m) - centre for k, m in enumerate(masses)]

    def row_sum(box, row, masses, left, right):
        acc = total(box)[row : row + 1]
        for m, l, r in zip(masses, left, right):
            acc = acc + m * l * r
        return acc

    lifted = lift(grad_hi[...].astype(F32))
    prob = probs[...]
    weighted_spread[...] = prob * local_moments(centre_box, prob, lifted)
    centre_box[me_m, 2:3] = jnp.concatenate(
        [folded(grad_piece, grad_piece), jnp.zeros((1, ROWS - 128), F32)], axis=1
    )
    swap_start(3, centre_box, me_m, at_m)
    swap_wait(3, centre_box, me_m, at_m)
    centre = total(centre_box)[0:1]
    logit_grad[...] = (count * (prob * (lifted - centre))).astype(BF16)
    masses, aways = row_aways(centre_box)
    first_y[y, 0:1] = lane_part(count * row_sum(centre_box, 1, masses, aways, aways))
    first_y[y, 1:2] = total(centre_box)[2:3, 0:128]
    swap_start(4, first_y, y, at_y)

    def pass_on():
        swap_wait(4, first_y, y, at_y)
        first_q[q] = total(first_y)
        swap_start(5, first_q, q, at_q)

    summed = scatter(1, send_a1, send_b1, y_a1, z_b1, pass_on, lambda: None)
    swap_wait(5, first_q, q, at_q)
    dots = jnp.sum(total(first_q), axis=1, keepdims=True)
    rr = dots[1:2]
    curvature = dots[0:1] / (SAMPLES * 64) + DAMPING * rr
    step = rr / curvature
    quad = step * step * curvature
    resid_piece = [
        g - step * (f / (SAMPLES * 64) + DAMPING * g) for f, g in zip(summed, grad_piece)
    ]
    keep(resid_hi, resid_piece)
    dots_m[me_m] = folded(resid_piece, resid_piece)
    swap_start(6, dots_m, me_m, at_m)
    gather_start(1, resid_hi)
    swap_wait(6, dots_m, me_m, at_m)
    dots_y[y] = total(dots_m)
    swap_start(7, dots_y, y, at_y)
    swap_wait(7, dots_y, y, at_y)
    gather_wait(1, resid_hi)

    lifted = lift(resid_hi[...].astype(F32))
    spread = local_moments(final_box, probs[...], lifted)
    final_box[me_m, 2:3] = jnp.sum(weighted_spread[...] * spread, axis=0, keepdims=True)
    swap_start(9, final_box, me_m, at_m)
    dots_q[q] = total(dots_y)
    swap_start(8, dots_q, q, at_q)
    gather_start(2, grad_lo)
    swap_wait(9, final_box, me_m, at_m)
    _, resid_aways = row_aways(final_box)
    curv_y[y, 0:1] = lane_part(count * row_sum(final_box, 1, masses, resid_aways, resid_aways))
    curv_y[y, 1:2] = lane_part(count * row_sum(final_box, 2, masses, resid_aways, aways))
    swap_start(10, curv_y, y, at_y)
    swap_wait(8, dots_q, q, at_q)
    rr_next = jnp.sum(total(dots_q), axis=1, keepdims=True)
    beta = rr_next / rr
    swap_wait(10, curv_y, y, at_y)
    curv_q[q] = total(curv_y)
    swap_start(11, curv_q, q, at_q)
    gather_wait(2, grad_lo)
    scatter_end(1, send_a1, send_b1)
    for n, full in enumerate((grad_hi, resid_hi, grad_lo)):
        gather_end(n, full)
    for k in range(16):
        part[k] = grad_hi[k].astype(F32) + grad_lo[k].astype(F32)
    for j in range(D // 128):
        cols = slice(128 * j, 128 * (j + 1))
        grad_t[cols] = part[:, :, cols].reshape(COLS, 128).T
        resid_t[cols] = resid_hi[:, :, cols].astype(F32).reshape(COLS, 128).T
    swap_wait(11, curv_q, q, at_q)
    curves = jnp.sum(total(curv_q), axis=1, keepdims=True)
    curvature = curves[0:1] + 2.0 * beta * curves[1:2] + beta * beta * dots[0:1]
    curvature = curvature / (SAMPLES * 64)
    curvature = curvature + DAMPING * (rr_next + beta * beta * rr)
    last = rr_next / curvature
    quad = quad + last * last * curvature
    scale = jnp.sqrt(D * A * RADIUS_SHARE / quad)
    of_grad = (step + last * beta) * scale
    of_resid = last * scale
    out[...] = of_grad * grad_t[...] + of_resid * resid_t[...]


def per_device(hidden, head, bias, ids, actions, rewards, values, starts, ratio, samples):
    dma = pltpu.SemaphoreType.DMA
    vmem = pltpu.VMEM

    def row(x):
        return x.reshape(1, -1)

    return pl.pallas_call(
        kernel,
        out_shape=jax.ShapeDtypeStruct((D, COLS), F32),
        in_specs=[pl.BlockSpec(memory_space=pltpu.MemorySpace.HBM)] * 10,
        out_specs=pl.BlockSpec(memory_space=pltpu.VMEM),
        scratch_shapes=[
            vmem((ROWS, D), BF16),
            vmem((D, COLS), BF16),
            vmem((AGENTS, COLS), F32),
            vmem((1, ROWS), jnp.int32),
            vmem((1, ROWS), jnp.int32),
            vmem((1, ROWS), F32),
            vmem((1, ROWS), F32),
            vmem((1, ROWS), jnp.int32),
            vmem((1, ROWS), F32),
            vmem((1, SAMPLES), jnp.int32),
            dma((10,)),
            vmem((COLS, ROWS), F32),
            vmem((COLS, ROWS), F32),
            vmem((COLS, ROWS), BF16),
            vmem((D, COLS), F32),
            vmem((D, COLS), F32),
            vmem((16, 8, D), F32),
            vmem((16, 8, D), BF16),
            vmem((16, 8, D), BF16),
            vmem((16, 8, D), BF16),
            vmem((8, 2, ROWS), F32),
            vmem((8, 3, ROWS), F32),
            vmem((8, 3, ROWS), F32),
            vmem((8, 2, 128), F32),
            vmem((8, 2, 128), F32),
            vmem((8, 1, 128), F32),
            vmem((8, 1, 128), F32),
            vmem((8, 1, 128), F32),
            vmem((8, 1, 128), F32),
            vmem((8, 1, 128), F32),
            vmem((8, 2, 128), F32),
            vmem((8, 2, 128), F32),
            vmem((2, NY, 8, LEFT), F32),
            vmem((2, NZ, 2, 8, D - LEFT), F32),
            vmem((NY, 8, LEFT), BF16),
            vmem((NZ, 2, 8, D - LEFT), BF16),
            vmem((NY, 8, LEFT), BF16),
            vmem((NZ, 2, 8, D - LEFT), BF16),
            vmem((NY, 8, LEFT), BF16),
            vmem((NZ, 2, 8, D - LEFT), BF16),
            vmem((NY, 8, LEFT), BF16),
            vmem((NZ, 2, 8, D - LEFT), BF16),
            vmem((2, NZ, 8, 384), F32),
            vmem((2, NY, 8, 256), F32),
            vmem((2, NZ, 8, 384), F32),
            vmem((2, NY, 8, 256), F32),
            vmem((NY, 8, LEFT), BF16),
            vmem((NZ, 2, 8, D - LEFT), BF16),
            vmem((NY, 8, LEFT), BF16),
            vmem((NZ, 2, 8, D - LEFT), BF16),
            vmem((NZ, 8, 384), BF16),
            vmem((NY, 8, 256), BF16),
            vmem((NZ, 8, 384), BF16),
            vmem((NY, 8, 256), BF16),
            dma((4,)),
            dma((4,)),
            dma((12,)),
            dma((12,)),
            dma((2, 6)),
            dma((2, 6)),
            dma((2, 12)),
            dma((3, 6)),
            dma((3, 4)),
            dma((3, 11)),
        ],
        compiler_params=pltpu.CompilerParams(
            collective_id=0, has_side_effects=True, vmem_limit_bytes=40 * 1024 * 1024
        ),
        name="step",
    )(
        *(
            pltpu.with_memory_space_constraint(x, pltpu.MemorySpace.HBM)
            for x in (
                hidden, head, bias, row(ids), row(actions), row(rewards), row(values), row(starts),
                row(ratio), row(samples),
            )
        )
    )


def solution(mesh):
    placed = (P("dp", None), P(None, "mp"), P(None, "mp")) + (P("dp"),) * 7
    return jax.shard_map(
        per_device, mesh=mesh, in_specs=placed, out_specs=P(None, "mp"), check_vma=False
    )
```

```python
import functools
import math

import jax
import jax.numpy as jnp
from jax import lax
from jax.experimental import pallas as pl
from jax.experimental.pallas import tpu as pltpu
from jax.sharding import PartitionSpec as P

D = 2560
A = 1024
AGENTS = 8
SEQ_LEN = 64
GAMMA = 0.99
TRACE_DECAY = 0.95
DAMPING = 0.001
RADIUS_SHARE = 0.001

MESH = pl.DeviceIdType.MESH
F32 = jnp.float32
BF16 = jnp.bfloat16
NY = 8
NZ = 4
NM = 8
ROWS = 512
SAMPLES = 2048
COLS = 128
LEFT = 1536
FAR_FIRST = (4, 3, 5, 2, 6, 1, 7)
NEAR_FIRST = (1, 7, 2, 6, 3, 5, 4)
ARRIVALS = (
    ("a", 1), ("a", 7), ("b", 1), ("a", 2), ("a", 6), ("b", 2), ("b", 3), ("a", 3), ("a", 5),
    ("a", 4),
)
CORE_ORDER = (
    ("a", 4), ("b", 3), ("a", 3), ("a", 5), ("b", 1), ("a", 2), ("a", 6), ("b", 2),
    ("a", 1), ("a", 7), ("a", 0), ("b", 0),
)


def kernel(
    hidden_in, head_in, bias_in, ids_in, actions_in, rewards_in, values_in, starts_in, ratio_in, samples_in,
    out,
    hidden, head, bias, ids, actions, rewards, values, starts, ratio, samples, loads,
    probs, weighted_spread, logit_grad, grad_t, resid_t, part, grad_hi, grad_lo, resid_hi,
    peak_box, centre_box, final_box, first_y, first_q, dots_m, dots_y, dots_q, adv_y, adv_q, curv_y, curv_q,
    core_a, core_b, send_a0, send_b0, y_a0, z_b0, send_a1, send_b1, y_a1, z_b1,
    own_a, own_b, z_a, y_b,
    rest_a, rest_b, rest_y, rest_z, rest_own_a, rest_own_b, rest_za, rest_yb, rest_s, rest_r,
    small_s, small_r, rs_s, rs_r, rs_core, ag_s, ag_r, ag_line,
):
    dp, me_m = lax.axis_index("dp"), lax.axis_index("mp")
    core = lax.rem(dp, 2)
    y = lax.rem(dp // 2, NY)
    z = dp // (2 * NY)
    q = z * 2 + core

    def at_y(k):
        return ((z * NY + k) * 2 + core, me_m)

    def at_q(k):
        return ((k // 2 * NY + y) * 2 + lax.rem(k, 2), me_m)

    def at_z(k):
        return ((k * NY + y) * 2 + core, me_m)

    def at_m(k):
        return (dp, k)

    other = (dp + 1 - 2 * core, me_m)

    barrier = pltpu.get_barrier_semaphore()
    for o in range(1, 8):
        for target in (
            at_y(lax.rem(y + o, NY)),
            at_q(lax.rem(q + o, 8)),
            at_m(lax.rem(me_m + o, NM)),
        ):
            pl.semaphore_signal(barrier, inc=1, device_id=target, device_id_type=MESH)

    fetches = [
        pltpu.make_async_copy(src, dst, loads.at[k])
        for k, (src, dst) in enumerate(
            (
                (rewards_in, rewards), (values_in, values), (starts_in, starts),
                (hidden_in, hidden), (head_in, head), (bias_in, bias), (ids_in, ids),
                (actions_in, actions), (ratio_in, ratio), (samples_in, samples),
            )
        )
    ]
    for fetch in fetches:
        fetch.start()

    def copy(src, dst, send, recv, target):
        return pltpu.make_async_remote_copy(
            src_ref=src, dst_ref=dst, send_sem=send, recv_sem=recv,
            device_id=target, device_id_type=MESH,
        )

    def wait_sent(view, sem):
        copy(view, view, sem, sem, other).wait_send()

    def wait_come(view, sem):
        copy(view, view, sem, sem, other).wait_recv()

    def swap_start(n, box, me, place):
        for o in range(1, 8):
            copy(
                box.at[me], box.at[me], small_s.at[n], small_r.at[n], place(lax.rem(me + o, 8))
            ).start()

    def swap_wait(n, box, me, place):
        wait_come(box.at[0:7], small_r.at[n])
        wait_sent(box.at[0:7], small_s.at[n])

    def total(box):
        acc = box[0]
        for k in range(1, 8):
            acc = acc + box[k]
        return acc

    def lane_part(row):
        return row[:, 0:128] + row[:, 128:256] + row[:, 256:384] + row[:, 384:512]

    for fetch in fetches[:3]:
        fetch.wait()

    def ahead(x, s):
        return pltpu.roll(x, ROWS - s, 1)

    def wide(ref):
        return jnp.broadcast_to(ref[...].astype(F32), (8, ROWS))

    position = lax.broadcasted_iota(jnp.int32, (8, ROWS), 1)
    value = wide(values)
    ends = (lax.rem(position, SEQ_LEN) == SEQ_LEN - 1) | (ahead(wide(starts), 1) > 0.5)
    continues = jnp.where(ends, 0.0, 1.0)
    advantage = wide(rewards) + GAMMA * continues * ahead(value, 1) - value
    keeps = GAMMA * TRACE_DECAY * continues
    for s in (1, 2, 4, 8, 16, 32):
        advantage = advantage + keeps * ahead(advantage, s)
        keeps = keeps * ahead(keeps, s)
    advantage = advantage[0:1]
    adv_y[y] = lane_part(advantage)

    for fetch in fetches[3:]:
        fetch.wait()

    logits = jnp.dot(hidden[...], head[...], preferred_element_type=F32).T
    bias_t = bias[...].T
    agent = ids[...]
    for k in range(AGENTS):
        logits = logits + jnp.where(agent == k, bias_t[:, k : k + 1], 0.0)
    peak = jnp.max(logits, axis=0, keepdims=True)
    exponent = jnp.exp(logits - peak)
    peak_box[me_m, 0:1] = peak
    peak_box[me_m, 1:2] = jnp.sum(exponent, axis=0, keepdims=True)
    probs[...] = exponent
    pl.semaphore_wait(barrier, 21)
    swap_start(0, adv_y, y, at_y)
    swap_start(1, peak_box, me_m, at_m)

    local = samples[...] - dp * ROWS
    high = lax.shift_right_logical(local, 7)
    low = lax.bitwise_and(local, 127)
    high_hot = (lax.broadcasted_iota(jnp.int32, (8, SAMPLES), 0) == high).astype(F32).astype(BF16)
    low_hot = (lax.broadcasted_iota(jnp.int32, (128, SAMPLES), 0) == low).astype(F32).astype(BF16)
    tally = lax.dot_general(
        high_hot, low_hot, (((1,), (1,)), ((), ())), preferred_element_type=F32
    )
    count = jnp.concatenate([tally[0:1], tally[1:2], tally[2:3], tally[3:4]], axis=1)

    swap_wait(0, adv_y, y, at_y)
    adv_q[q] = total(adv_y)
    swap_start(2, adv_q, q, at_q)

    swap_wait(1, peak_box, me_m, at_m)
    row_peak = peak_box[0, 0:1]
    for k in range(1, NM):
        row_peak = jnp.maximum(row_peak, peak_box[k, 0:1])
    denominator = peak_box[0, 1:2] * jnp.exp(peak_box[0, 0:1] - row_peak)
    for k in range(1, NM):
        denominator = denominator + peak_box[k, 1:2] * jnp.exp(peak_box[k, 0:1] - row_peak)
    prob = probs[...] * (jnp.exp(peak - row_peak) / denominator)
    probs[...] = prob

    swap_wait(2, adv_q, q, at_q)
    tokens = ROWS * 64
    adv_mean = jnp.sum(total(adv_q), axis=1, keepdims=True) / tokens
    weight = ratio[...] * (advantage - adv_mean) / tokens
    picked = lax.broadcasted_iota(jnp.int32, (COLS, ROWS), 0) == actions[...] - me_m * COLS
    logit_grad[...] = (weight * (jnp.where(picked, 1.0, 0.0) - prob)).astype(BF16)

    def project(tiles):
        for j in tiles:
            cols = slice(512 * j, 512 * (j + 1))
            part[:, :, cols] = jnp.dot(
                logit_grad[...], hidden[:, cols], preferred_element_type=F32
            ).reshape(16, 8, 512)

    def scatter(n, send_a, send_b, y_a, z_b, between, then):
        def core_copy(kind, o):
            if kind == "a":
                k = (1 - core) * 8 + lax.rem(y + o, NY)
                return copy(
                    part.at[k, :, 0:LEFT], core_a.at[n, o], rs_s.at[n, 0], rs_core.at[n, o], other
                )
            k = (1 - core) * 8 + lax.rem(z + o, NZ) * 2
            return copy(
                part.at[pl.ds(k, 2), :, LEFT:D], core_b.at[n, o],
                rs_s.at[n, 1], rs_core.at[n, 8 + o], other,
            )

        for tiles, part_kind in ((range(3), "a"), (range(3, 5), "b")):
            project(tiles)
            for kind, o in CORE_ORDER:
                if kind == part_kind:
                    core_copy(kind, o).start()
        for kind, o in CORE_ORDER:
            core_copy(kind, o).wait_recv()
            if kind == "a":
                k = lax.rem(y + o, NY)
                term = part[core * 8 + k, :, 0:LEFT] + core_a[n, o]
                if o == 0:
                    acc_a = term
                    continue
                send_a[o] = term.astype(BF16)
                if n == 0:
                    rest_a[o] = (term - term.astype(BF16).astype(F32)).astype(BF16)
                copy(send_a.at[o], y_a.at[o], rs_s.at[n, 2], rs_r.at[n, 2], at_y(k)).start()
            else:
                k = lax.rem(z + o, NZ)
                term = part[pl.ds(core * 8 + 2 * k, 2), :, LEFT:D] + core_b[n, o]
                if o == 0:
                    acc_b = term
                    continue
                send_b[o] = term.astype(BF16)
                if n == 0:
                    rest_b[o] = (term - term.astype(BF16).astype(F32)).astype(BF16)
                copy(send_b.at[o], z_b.at[o], rs_s.at[n, 3], rs_r.at[n, 3], at_z(k)).start()
        wait_come(z_b.at[1:4], rs_r.at[n, 3])
        for o in (1, 2, 3):
            acc_b = acc_b + z_b[o].astype(F32)
        for k in range(NY):
            own_b[n, k] = acc_b[k // 4, :, 256 * (k % 4) : 256 * (k % 4 + 1)]
        for o in FAR_FIRST:
            k = lax.rem(y + o, NY)
            copy(own_b.at[n, k], y_b.at[n, o], rs_s.at[n, 4], rs_r.at[n, 4], at_y(k)).start()
        between()
        wait_come(y_a.at[1:8], rs_r.at[n, 2])
        for o in NEAR_FIRST:
            acc_a = acc_a + y_a[o].astype(F32)
        for k in range(NZ):
            own_a[n, k] = acc_a[:, 384 * k : 384 * (k + 1)]
        for o in (3, 2, 1):
            k = lax.rem(z + o, NZ)
            copy(own_a.at[n, k], z_a.at[n, o], rs_s.at[n, 5], rs_r.at[n, 5], at_z(k)).start()
        then()
        shard_b = own_b[n, y]
        wait_come(y_b.at[n, 1:8], rs_r.at[n, 4])
        for o in NEAR_FIRST:
            shard_b = shard_b + y_b[n, o]
        shard_a = own_a[n, z]
        wait_come(z_a.at[n, 1:4], rs_r.at[n, 5])
        for o in (1, 2, 3):
            shard_a = shard_a + z_a[n, o]
        return shard_a, shard_b

    def rest_start():
        for o in FAR_FIRST:
            copy(
                rest_a.at[o], rest_y.at[o], rest_s.at[0], rest_r.at[0], at_y(lax.rem(y + o, NY))
            ).start()
        for o in (3, 2, 1):
            copy(
                rest_b.at[o], rest_z.at[o], rest_s.at[1], rest_r.at[1], at_z(lax.rem(z + o, NZ))
            ).start()

    def rest_turn():
        wait_come(rest_z.at[1:4], rest_r.at[1])
        acc = rest_z[1].astype(F32) + rest_z[2].astype(F32) + rest_z[3].astype(F32)
        for k in range(NY):
            cols = slice(256 * (k % 4), 256 * (k % 4 + 1))
            rest_own_b[k] = acc[k // 4, :, cols].astype(BF16)
        for o in FAR_FIRST:
            k = lax.rem(y + o, NY)
            copy(rest_own_b.at[k], rest_yb.at[o], rest_s.at[2], rest_r.at[2], at_y(k)).start()
        wait_come(rest_y.at[1:8], rest_r.at[0])
        acc = rest_y[1].astype(F32)
        for o in range(2, 8):
            acc = acc + rest_y[o].astype(F32)
        for k in range(NZ):
            rest_own_a[k] = acc[:, 384 * k : 384 * (k + 1)].astype(BF16)
        for o in (3, 2, 1):
            k = lax.rem(z + o, NZ)
            copy(rest_own_a.at[k], rest_za.at[o], rest_s.at[3], rest_r.at[3], at_z(k)).start()

    def rest_wait():
        rest_of_b = rest_own_b[y].astype(F32)
        wait_come(rest_yb.at[1:8], rest_r.at[2])
        for o in range(1, 8):
            rest_of_b = rest_of_b + rest_yb[o].astype(F32)
        rest_of_a = rest_own_a[z].astype(F32)
        wait_come(rest_za.at[1:4], rest_r.at[3])
        for o in range(1, 4):
            rest_of_a = rest_of_a + rest_za[o].astype(F32)
        wait_sent(rest_a.at[1:8], rest_s.at[0])
        wait_sent(rest_b.at[1:4], rest_s.at[1])
        wait_sent(rest_own_b.at[1:8], rest_s.at[2])
        wait_sent(rest_own_a.at[1:4], rest_s.at[3])
        return rest_of_a, rest_of_b

    def scatter_end(n, send_a, send_b):
        wait_sent(part.at[0:8, :, 0:LEFT], rs_s.at[n, 0])
        wait_sent(part.at[0:8, :, LEFT:D], rs_s.at[n, 1])
        wait_sent(send_a.at[1:8], rs_s.at[n, 2])
        wait_sent(send_b.at[1:4], rs_s.at[n, 3])
        wait_sent(own_b.at[n, 1:8], rs_s.at[n, 4])
        wait_sent(own_a.at[n, 1:4], rs_s.at[n, 5])

    def spot_a(full, ky, kz):
        return full.at[core * 8 + ky, :, pl.ds(pl.multiple_of(kz * 384, 128), 384)]

    def spot_b(full, ky, kz):
        columns = pl.ds(pl.multiple_of(LEFT + lax.rem(ky, 4) * 256, 128), 256)
        return full.at[core * 8 + 2 * kz + ky // 4, :, columns]

    def line_a(full, kc, ky):
        return full.at[kc * 8 + ky, :, 0:LEFT]

    def line_b(full, kc, kz):
        return full.at[pl.ds(kc * 8 + 2 * kz, 2), :, LEFT:D]

    def gather_start(n, full):
        def begin(ref, kind, recv, target):
            copy(ref, ref, ag_s.at[n, kind], recv, target).start()

        mine = core * 8 + y
        for o in (3, 2, 1):
            begin(spot_a(full, y, z), 0, ag_r.at[n, 0], at_z(lax.rem(z + o, NZ)))
        for o in FAR_FIRST:
            begin(spot_b(full, y, z), 1, ag_r.at[n, 1], at_y(lax.rem(y + o, NY)))
        wait_come(full.at[mine, :, 0 : 3 * 384], ag_r.at[n, 0])
        for o in FAR_FIRST:
            begin(line_a(full, core, y), 2, ag_line.at[n, o], at_y(lax.rem(y + o, NY)))
        begin(line_a(full, core, y), 4, ag_r.at[n, 2], other)
        wait_come(full.at[mine, :, 0 : 7 * 256], ag_r.at[n, 1])
        for o in (3, 2, 1):
            begin(line_b(full, core, z), 3, ag_line.at[n, 7 + o], at_z(lax.rem(z + o, NZ)))
        begin(line_b(full, core, z), 5, ag_r.at[n, 3], other)

    def gather_wait(n, full):
        def arrive(ref, line, kind, recv):
            wait_come(ref, ag_line.at[n, line])
            copy(ref, ref, ag_s.at[n, kind], recv, other).start()

        for kind, o in ARRIVALS:
            if kind == "a":
                arrive(line_a(full, core, lax.rem(y + NY - o, NY)), o, 4, ag_r.at[n, 2])
            else:
                arrive(line_b(full, core, lax.rem(z + NZ - o, NZ)), 7 + o, 5, ag_r.at[n, 3])
        wait_come(full.at[pl.ds((1 - core) * 8, 8), :, 0:LEFT], ag_r.at[n, 2])
        wait_come(full.at[pl.ds((1 - core) * 8, 8), :, LEFT:D], ag_r.at[n, 3])

    def gather_end(n, full):
        wait_sent(full.at[0, :, 0 : 3 * 384], ag_s.at[n, 0])
        wait_sent(full.at[0, :, 0 : 7 * 256], ag_s.at[n, 1])
        wait_sent(full.at[0:7, :, 0:LEFT], ag_s.at[n, 2])
        wait_sent(full.at[0:6, :, LEFT:D], ag_s.at[n, 3])
        wait_sent(full.at[0:8, :, 0:LEFT], ag_s.at[n, 4])
        wait_sent(full.at[0:8, :, LEFT:D], ag_s.at[n, 5])

    def keep(full, shards):
        shard_a, shard_b = shards
        full[core * 8 + y, :, pl.ds(pl.multiple_of(z * 384, 128), 384)] = shard_a.astype(BF16)
        columns = pl.ds(pl.multiple_of(LEFT + lax.rem(y, 4) * 256, 128), 256)
        full[core * 8 + 2 * z + y // 4, :, columns] = shard_b.astype(BF16)

    def lift(vector):
        return lax.dot_general(
            vector.reshape(COLS, D).astype(BF16), hidden[...], (((1,), (1,)), ((), ())),
            preferred_element_type=F32,
        )

    def folded(left, right):
        terms = [
            l[:, k : k + 128] * r[:, k : k + 128]
            for l, r in zip(left, right)
            for k in range(0, l.shape[1], 128)
        ]
        return jnp.sum(sum(terms[1:], terms[0]), axis=0, keepdims=True)

    grad_first = scatter(0, send_a0, send_b0, y_a0, z_b0, lambda: None, rest_start)
    keep(grad_hi, grad_first)
    gather_start(0, grad_hi)
    rest_turn()
    gather_wait(0, grad_hi)
    scatter_end(0, send_a0, send_b0)
    grad_piece = [x + r for x, r in zip(grad_first, rest_wait())]
    keep(grad_lo, [x - f.astype(BF16).astype(F32) for x, f in zip(grad_piece, grad_first)])

    def local_moments(box, prob, lifted):
        mass = jnp.sum(prob, axis=0, keepdims=True)
        moment = jnp.sum(prob * lifted, axis=0, keepdims=True)
        spread = lifted - share(moment, mass)
        box[me_m, 0:1] = moment
        box[me_m, 1:2] = jnp.sum(prob * spread * spread, axis=0, keepdims=True)
        return spread

    def share(moment, mass):
        return jnp.where(mass > 0.0, moment / jnp.where(mass > 0.0, mass, 1.0), 0.0)

    def row_aways(box):
        masses = [
            peak_box[k, 1:2] * (jnp.exp(peak_box[k, 0:1] - row_peak) / denominator)
            for k in range(NM)
        ]
        centre = total(box)[0:1]
        return masses, [share(box[k, 0:1], m) - centre for k, m in enumerate(masses)]

    def row_sum(box, row, masses, left, right):
        acc = total(box)[row : row + 1]
        for m, l, r in zip(masses, left, right):
            acc = acc + m * l * r
        return acc

    lifted = lift(grad_hi[...].astype(F32))
    prob = probs[...]
    weighted_spread[...] = prob * local_moments(centre_box, prob, lifted)
    centre_box[me_m, 2:3] = jnp.concatenate(
        [folded(grad_piece, grad_piece), jnp.zeros((1, ROWS - 128), F32)], axis=1
    )
    swap_start(3, centre_box, me_m, at_m)
    gather_start(2, grad_lo)
    swap_wait(3, centre_box, me_m, at_m)
    centre = total(centre_box)[0:1]
    logit_grad[...] = (count * (prob * (lifted - centre))).astype(BF16)
    masses, aways = row_aways(centre_box)
    first_y[y, 0:1] = lane_part(count * row_sum(centre_box, 1, masses, aways, aways))
    first_y[y, 1:2] = total(centre_box)[2:3, 0:128]
    swap_start(4, first_y, y, at_y)

    def pass_on():
        swap_wait(4, first_y, y, at_y)
        first_q[q] = total(first_y)
        swap_start(5, first_q, q, at_q)

    summed = scatter(1, send_a1, send_b1, y_a1, z_b1, pass_on, lambda: None)
    swap_wait(5, first_q, q, at_q)
    dots = jnp.sum(total(first_q), axis=1, keepdims=True)
    rr = dots[1:2]
    curvature = dots[0:1] / (SAMPLES * 64) + DAMPING * rr
    step = rr / curvature
    quad = step * step * curvature
    resid_piece = [
        g - step * (f / (SAMPLES * 64) + DAMPING * g) for f, g in zip(summed, grad_piece)
    ]
    keep(resid_hi, resid_piece)
    dots_m[me_m] = folded(resid_piece, resid_piece)
    swap_start(6, dots_m, me_m, at_m)
    gather_start(1, resid_hi)
    swap_wait(6, dots_m, me_m, at_m)
    dots_y[y] = total(dots_m)
    swap_start(7, dots_y, y, at_y)
    swap_wait(7, dots_y, y, at_y)
    gather_wait(1, resid_hi)

    lifted = lift(resid_hi[...].astype(F32))
    spread = local_moments(final_box, probs[...], lifted)
    final_box[me_m, 2:3] = jnp.sum(weighted_spread[...] * spread, axis=0, keepdims=True)
    swap_start(9, final_box, me_m, at_m)
    dots_q[q] = total(dots_y)
    swap_start(8, dots_q, q, at_q)
    swap_wait(9, final_box, me_m, at_m)
    _, resid_aways = row_aways(final_box)
    curv_y[y, 0:1] = lane_part(count * row_sum(final_box, 1, masses, resid_aways, resid_aways))
    curv_y[y, 1:2] = lane_part(count * row_sum(final_box, 2, masses, resid_aways, aways))
    swap_start(10, curv_y, y, at_y)
    swap_wait(8, dots_q, q, at_q)
    rr_next = jnp.sum(total(dots_q), axis=1, keepdims=True)
    beta = rr_next / rr
    swap_wait(10, curv_y, y, at_y)
    curv_q[q] = total(curv_y)
    swap_start(11, curv_q, q, at_q)
    gather_wait(2, grad_lo)
    scatter_end(1, send_a1, send_b1)
    for n, full in enumerate((grad_hi, resid_hi, grad_lo)):
        gather_end(n, full)
    for k in range(16):
        part[k] = grad_hi[k].astype(F32) + grad_lo[k].astype(F32)
    for j in range(D // 128):
        cols = slice(128 * j, 128 * (j + 1))
        grad_t[cols] = part[:, :, cols].reshape(COLS, 128).T
        resid_t[cols] = resid_hi[:, :, cols].astype(F32).reshape(COLS, 128).T
    swap_wait(11, curv_q, q, at_q)
    curves = jnp.sum(total(curv_q), axis=1, keepdims=True)
    curvature = curves[0:1] + 2.0 * beta * curves[1:2] + beta * beta * dots[0:1]
    curvature = curvature / (SAMPLES * 64)
    curvature = curvature + DAMPING * (rr_next + beta * beta * rr)
    last = rr_next / curvature
    quad = quad + last * last * curvature
    scale = jnp.sqrt(D * A * RADIUS_SHARE / quad)
    of_grad = (step + last * beta) * scale
    of_resid = last * scale
    out[...] = of_grad * grad_t[...] + of_resid * resid_t[...]


def per_device(hidden, head, bias, ids, actions, rewards, values, starts, ratio, samples):
    dma = pltpu.SemaphoreType.DMA
    vmem = pltpu.VMEM

    def row(x):
        return x.reshape(1, -1)

    return pl.pallas_call(
        kernel,
        out_shape=jax.ShapeDtypeStruct((D, COLS), F32),
        in_specs=[pl.BlockSpec(memory_space=pltpu.MemorySpace.HBM)] * 10,
        out_specs=pl.BlockSpec(memory_space=pltpu.VMEM),
        scratch_shapes=[
            vmem((ROWS, D), BF16),
            vmem((D, COLS), BF16),
            vmem((AGENTS, COLS), F32),
            vmem((1, ROWS), jnp.int32),
            vmem((1, ROWS), jnp.int32),
            vmem((1, ROWS), F32),
            vmem((1, ROWS), F32),
            vmem((1, ROWS), jnp.int32),
            vmem((1, ROWS), F32),
            vmem((1, SAMPLES), jnp.int32),
            dma((10,)),
            vmem((COLS, ROWS), F32),
            vmem((COLS, ROWS), F32),
            vmem((COLS, ROWS), BF16),
            vmem((D, COLS), F32),
            vmem((D, COLS), F32),
            vmem((16, 8, D), F32),
            vmem((16, 8, D), BF16),
            vmem((16, 8, D), BF16),
            vmem((16, 8, D), BF16),
            vmem((8, 2, ROWS), F32),
            vmem((8, 3, ROWS), F32),
            vmem((8, 3, ROWS), F32),
            vmem((8, 2, 128), F32),
            vmem((8, 2, 128), F32),
            vmem((8, 1, 128), F32),
            vmem((8, 1, 128), F32),
            vmem((8, 1, 128), F32),
            vmem((8, 1, 128), F32),
            vmem((8, 1, 128), F32),
            vmem((8, 2, 128), F32),
            vmem((8, 2, 128), F32),
            vmem((2, NY, 8, LEFT), F32),
            vmem((2, NZ, 2, 8, D - LEFT), F32),
            vmem((NY, 8, LEFT), BF16),
            vmem((NZ, 2, 8, D - LEFT), BF16),
            vmem((NY, 8, LEFT), BF16),
            vmem((NZ, 2, 8, D - LEFT), BF16),
            vmem((NY, 8, LEFT), BF16),
            vmem((NZ, 2, 8, D - LEFT), BF16),
            vmem((NY, 8, LEFT), BF16),
            vmem((NZ, 2, 8, D - LEFT), BF16),
            vmem((2, NZ, 8, 384), F32),
            vmem((2, NY, 8, 256), F32),
            vmem((2, NZ, 8, 384), F32),
            vmem((2, NY, 8, 256), F32),
            vmem((NY, 8, LEFT), BF16),
            vmem((NZ, 2, 8, D - LEFT), BF16),
            vmem((NY, 8, LEFT), BF16),
            vmem((NZ, 2, 8, D - LEFT), BF16),
            vmem((NZ, 8, 384), BF16),
            vmem((NY, 8, 256), BF16),
            vmem((NZ, 8, 384), BF16),
            vmem((NY, 8, 256), BF16),
            dma((4,)),
            dma((4,)),
            dma((12,)),
            dma((12,)),
            dma((2, 6)),
            dma((2, 6)),
            dma((2, 12)),
            dma((3, 6)),
            dma((3, 4)),
            dma((3, 11)),
        ],
        compiler_params=pltpu.CompilerParams(
            collective_id=0, has_side_effects=True, vmem_limit_bytes=40 * 1024 * 1024
        ),
        name="step",
    )(
        *(
            pltpu.with_memory_space_constraint(x, pltpu.MemorySpace.HBM)
            for x in (
                hidden, head, bias, row(ids), row(actions), row(rewards), row(values), row(starts),
                row(ratio), row(samples),
            )
        )
    )


def solution(mesh):
    placed = (P("dp", None), P(None, "mp"), P(None, "mp")) + (P("dp"),) * 7
    return jax.shard_map(
        per_device, mesh=mesh, in_specs=placed, out_specs=P(None, "mp"), check_vma=False
    )
```
